256 devices in a mesh: ctx: 32 (over x, z), head: 8 (over y, core).
Axes of the slice: x: 4, y: 4, z: 8, core: 2. Of those that a mesh axis runs over, the one named last changes fastest.
Arguments:
- layer_input: bfloat16 [16384, 8192], P('ctx', 'head'), may hold values from -6 to 6
- query_columns: bfloat16 [16384, 8192], P('ctx', 'head'), may hold values from -6 to 6
- key_columns: bfloat16 [16384, 1024], P('ctx', 'head'), may hold values from -6 to 6
- value_columns: bfloat16 [16384, 1024], P('ctx', 'head'), may hold values from -6 to 6
- output_gradient: bfloat16 [16384, 8192], P('ctx', 'head'), may hold values from -6 to 6
Outputs:
- query_grad: bfloat16 [16384, 8192], P('ctx', 'head')
- key_weight_grad: float32 [8192, 1024], P(('head', 'ctx'))
- value_weight_grad: float32 [8192, 1024], P(('head', 'ctx'))
The draws below stay inside these ranges and needn't reach their ends.
All inputs are finite; a program needn't handle non-finite values.
Results may differ from the reference program's by a relative error of at most 0.014.
Values may be sent and summed in bfloat16 or wider, within the bound.
A program may use at most 128 MiB of HBM per device.

```python
import jax
import jax.numpy as jnp
from jax import lax

D = 8192
QUERY_HEADS = 64
KEY_VALUE_HEADS = 8
HEAD_SIZE = 128
BLOCK_TOKENS = 256
DOCUMENT_TOKENS = 16384


def raised(values, key, source, target, shards_of, factor):
    owner, partner = [(jnp.arange(values.shape[position]) // (values.shape[position] // shards_of)).reshape([-1 if axis == position else 1 for axis in range(values.ndim)]) for position in (source, target)]
    chosen = jax.random.permutation(key, shards_of)[partner]
    strong = (owner == chosen) | (owner == (partner + shards_of // 2) % shards_of)
    return jnp.where(strong, factor * values, values)


def block_levels(own_key, dims, pieces, low, top_value):
    def one(dim, parts):
        heights = jax.random.uniform(jax.random.fold_in(jax.random.fold_in(own_key, 6), dim), (parts,), jnp.float32, low / len(pieces), top_value / len(pieces))
        return jnp.repeat(jnp.exp(heights), dims[dim] // parts).reshape((-1,) + (1,) * (len(dims) - dim - 1))

    loudness = one(*pieces[0])
    for cut in pieces[1:]:
        loudness = loudness * one(*cut)
    return loudness


def normal_values(stream_key, dims, width, reach, split=(), kind=jnp.bfloat16):
    drawn = jax.random.normal(stream_key, dims, jnp.float32) * width
    if len(split) > 0:
        drawn = block_levels(stream_key, dims, split, -0.22, 0.18) * drawn
    return jnp.clip(drawn, min=-reach, max=reach).astype(kind)


def gaussian_with(key, extent, width, bound, pieces, heavy, dtype=jnp.bfloat16):
    values = width * jax.random.normal(key, extent, jnp.float32)
    if pieces:
        values = values * block_levels(key, extent, pieces, -0.22, 0.18)
    return jnp.clip(raised(values, jax.random.fold_in(key, 3), *heavy), -bound, bound).astype(dtype)


def setup_inputs(seed: int = 0) -> dict:
    streams_of = jax.random.split(jax.random.key(seed), 6)
    layer_input = gaussian_with(streams_of[0], (DOCUMENT_TOKENS, D), 1.0, 6.0, ((0, 32), (1, 8)), (0, 1, 32, 2.75))
    query_columns = normal_values(streams_of[1], (DOCUMENT_TOKENS, QUERY_HEADS * HEAD_SIZE), 1.0, 6.0, ((0, 32), (1, 8)))
    key_columns = normal_values(streams_of[2], (DOCUMENT_TOKENS, KEY_VALUE_HEADS * HEAD_SIZE), 1.0, 6.0, ((0, 32), (1, 8)))
    value_columns = normal_values(streams_of[3], (DOCUMENT_TOKENS, KEY_VALUE_HEADS * HEAD_SIZE), 1.0, 6.0, ((0, 32), (1, 8)))
    output_gradient = normal_values(streams_of[4], (DOCUMENT_TOKENS, QUERY_HEADS * HEAD_SIZE), 1.0, 6.0, ((0, 32), (1, 8)))
    return dict(layer_input=layer_input, query_columns=query_columns, key_columns=key_columns, value_columns=value_columns, output_gradient=output_gradient)


highest = lax.Precision.HIGHEST


def positive_features(raw):
    wide = raw.astype(jnp.float32)
    return jnp.where(wide > 0, wide + 1.0, jnp.exp(jnp.minimum(wide, 0.0))).astype(jnp.bfloat16)


def feature_derivative(raw):
    wide = raw.astype(jnp.float32)
    return jnp.where(wide > 0, 1.0, jnp.exp(jnp.minimum(wide, 0.0)))


def causal_mask(length):
    rows_at = lax.broadcasted_iota(jnp.int32, (length, length), 0)
    cols_at = lax.broadcasted_iota(jnp.int32, (length, length), 1)
    return cols_at <= rows_at


def block_states(key_features, value_entries):
    states = jnp.einsum('ske,skf->kef', key_features, value_entries, preferred_element_type=jnp.float32)
    totals = jnp.sum(key_features.astype(jnp.float32), axis=0)
    return states, totals


def block_scores(query_features, key_features):
    attention_scores = jnp.einsum('tkge,ske->kgts', query_features, key_features, preferred_element_type=jnp.float32)
    return jnp.where(causal_mask(attention_scores.shape[-1]), attention_scores, jnp.float32(0.0))


def forward_blockwise_pass(query_features, value_entries, output_cotangent, prior_state, prior_total, attention_scores):
    query_wide = query_features.astype(jnp.float32)
    denom = jnp.einsum('tkge,ke->tkg', query_wide, prior_total, precision=highest) + jnp.transpose(jnp.sum(attention_scores, axis=-1), (2, 0, 1))
    numer = jnp.einsum('tkge,kef->tkgf', query_wide, prior_state, precision=highest) + jnp.einsum('kgts,skf->tkgf', attention_scores.astype(jnp.bfloat16), value_entries, preferred_element_type=jnp.float32)
    output = numer / denom[..., None]
    wide_cot = output_cotangent.astype(jnp.float32)
    scaled = (wide_cot / denom[..., None]).astype(jnp.bfloat16)
    weight = -jnp.sum(wide_cot * output, axis=-1) / denom
    grad_state = jnp.einsum('tkge,tkgf->kef', query_features, scaled, preferred_element_type=jnp.float32)
    grad_total = jnp.einsum('tkge,tkg->ke', query_wide, weight, precision=highest)
    return scaled, weight, grad_state, grad_total


def backward_blockwise_pass(query_features, key_features, value_entries, lower_triangle_scores, scaled, weight, prior_state, prior_total, later_state, later_total):
    dscores = jnp.einsum('tkgf,skf->kgts', scaled, value_entries, preferred_element_type=jnp.float32) + jnp.transpose(weight, (1, 2, 0))[..., None]
    dscores = jnp.where(causal_mask(dscores.shape[-1]), dscores, jnp.float32(0.0)).astype(jnp.bfloat16)
    grad_query = jnp.einsum('tkgf,kef->tkge', scaled.astype(jnp.float32), prior_state, precision=highest) + weight[..., None] * prior_total[None, :, None, :] + jnp.einsum('kgts,ske->tkge', dscores, key_features, preferred_element_type=jnp.float32)
    key_gradient_rows = jnp.einsum('kgts,tkge->ske', dscores, query_features, preferred_element_type=jnp.float32) + jnp.einsum('kef,skf->ske', later_state, value_entries.astype(jnp.float32), precision=highest) + later_total[None]
    value_gradient_rows = jnp.einsum('kgts,tkgf->skf', lower_triangle_scores, scaled, preferred_element_type=jnp.float32) + jnp.einsum('kef,ske->skf', later_state, key_features.astype(jnp.float32), precision=highest)
    return grad_query, key_gradient_rows, value_gradient_rows


def exclusive_prefix(stack):
    running = jnp.cumsum(stack, axis=0)
    return jnp.concatenate([jnp.zeros_like(stack[:1]), running[:-1]], axis=0)


def exclusive_suffix(stack):
    running = jnp.cumsum(stack[::-1], axis=0)[::-1]
    return jnp.concatenate([running[1:], jnp.zeros_like(stack[:1])], axis=0)


def reference(layer_input, query_columns, key_columns, value_columns, output_gradient):
    query_group_count = QUERY_HEADS // KEY_VALUE_HEADS
    block_count = DOCUMENT_TOKENS // BLOCK_TOKENS
    query_features = positive_features(query_columns).reshape(block_count, BLOCK_TOKENS, KEY_VALUE_HEADS, query_group_count, HEAD_SIZE)
    key_features = positive_features(key_columns).reshape(block_count, BLOCK_TOKENS, KEY_VALUE_HEADS, HEAD_SIZE)
    value_entries = value_columns.reshape(block_count, BLOCK_TOKENS, KEY_VALUE_HEADS, HEAD_SIZE)
    output_cotangent = output_gradient.reshape(block_count, BLOCK_TOKENS, KEY_VALUE_HEADS, query_group_count, HEAD_SIZE)
    states, totals = jax.vmap(block_states)(key_features, value_entries)
    prior_state = exclusive_prefix(states)
    prior_total = exclusive_prefix(totals)

    def forward_one(block_entries):
        query_block, key_block, value_block, cotangent_block, prior_block_state, prior_block_total = block_entries
        attention_scores = block_scores(query_block, key_block)
        return forward_blockwise_pass(query_block, value_block, cotangent_block, prior_block_state, prior_block_total, attention_scores)

    scaled, weight, grad_states, grad_totals = lax.map(forward_one, (query_features, key_features, value_entries, output_cotangent, prior_state, prior_total))
    later_state = exclusive_suffix(grad_states)
    later_total = exclusive_suffix(grad_totals)

    def backward_one(block_entries):
        query_block, key_block, value_block, score_block, weight_block, prior_block_state, prior_block_total, later_block_state, later_block_total = block_entries
        lower_triangle_scores = block_scores(query_block, key_block).astype(jnp.bfloat16)
        return backward_blockwise_pass(query_block, key_block, value_block, lower_triangle_scores, score_block, weight_block, prior_block_state, prior_block_total, later_block_state, later_block_total)

    grad_query, key_gradient_rows, value_gradient_rows = lax.map(backward_one, (query_features, key_features, value_entries, scaled, weight, prior_state, prior_total, later_state, later_total))
    query_grad = (grad_query.reshape(DOCUMENT_TOKENS, QUERY_HEADS * HEAD_SIZE) * feature_derivative(query_columns)).astype(jnp.bfloat16)
    key_gradient = (key_gradient_rows.reshape(DOCUMENT_TOKENS, KEY_VALUE_HEADS * HEAD_SIZE) * feature_derivative(key_columns)).astype(jnp.bfloat16)
    value_gradient = value_gradient_rows.reshape(DOCUMENT_TOKENS, KEY_VALUE_HEADS * HEAD_SIZE).astype(jnp.bfloat16)
    key_weight_grad = jnp.dot(layer_input.T, key_gradient, preferred_element_type=jnp.float32)
    value_weight_grad = jnp.dot(layer_input.T, value_gradient, preferred_element_type=jnp.float32)
    return query_grad, key_weight_grad, value_weight_grad
```

```python
import jax
import jax.numpy as jnp
from jax import lax
from jax.experimental import pallas as pl
from jax.experimental.pallas import tpu as pltpu
from jax.sharding import PartitionSpec as P

QUERY_HEADS = 64
KEY_VALUE_HEADS = 8
GROUP = QUERY_HEADS // KEY_VALUE_HEADS
HEAD = 128
BLOCK = 256
ROWS = 512
CTX = 32
XS = 4
ZS = 8
YS = 4
PART = HEAD // CTX
MESH = pl.DeviceIdType.MESH
F32 = jnp.float32
BF16 = jnp.bfloat16
VMEM = pl.BlockSpec(memory_space=pltpu.VMEM)


def phi(raw):
    wide = raw.astype(F32)
    return jnp.where(wide > 0, wide + 1.0, jnp.exp(jnp.minimum(wide, 0.0))).astype(BF16)


def slope(raw):
    wide = raw.astype(F32)
    return jnp.where(wide > 0, 1.0, jnp.exp(jnp.minimum(wide, 0.0)))


def dot_nn(a, b):
    return lax.dot_general(a, b, (((1,), (0,)), ((), ())), preferred_element_type=F32)


def dot_nt(a, b):
    return lax.dot_general(a, b, (((1,), (1,)), ((), ())), preferred_element_type=F32)


def dot_tn(a, b):
    return lax.dot_general(a, b, (((0,), (0,)), ((), ())), preferred_element_type=F32)


def halves(value):
    high = value.astype(BF16)
    return high, (value - high.astype(F32)).astype(BF16)


def lower_mask():
    rows = lax.broadcasted_iota(jnp.int32, (BLOCK, BLOCK), 0)
    cols = lax.broadcasted_iota(jnp.int32, (BLOCK, BLOCK), 1)
    return cols <= rows


def spread_copy(source, target, send, recv, me, k):
    peer = lax.rem(me + k, CTX)
    return pltpu.make_async_remote_copy(
        src_ref=source.at[peer],
        dst_ref=target.at[me],
        send_sem=send.at[k],
        recv_sem=recv.at[k],
        device_id={"ctx": peer},
        device_id_type=MESH,
    )


def spread_start(source, target, send, recv, me):
    def one(k, carry):
        spread_copy(source, target, send, recv, me, k).start()
        return carry

    lax.fori_loop(1, CTX, one, 0)
    target[me] = source[me]


def spread_wait(source, target, send, recv, me):
    def one(k, carry):
        copy = spread_copy(source, target, send, recv, me, k)
        copy.wait_recv()
        copy.wait_send()
        return carry

    lax.fori_loop(1, CTX, one, 0)


def fill_parts(mine, state, total):
    for part in range(CTX):
        mine[part, 0:PART, :] = state[part * PART : (part + 1) * PART, :]
        mine[part, PART : 2 * PART, :] = jnp.broadcast_to(total, (PART, HEAD))


def running(inbox, outbox, reverse):
    total = jnp.zeros((2 * PART, HEAD), F32)
    for step in range(CTX):
        at = CTX - 1 - step if reverse else step
        outbox[at] = total
        total = total + inbox[at]


def join_parts(got, state):
    for part in range(CTX):
        state[part * PART : (part + 1) * PART, :] = got[part, 0:PART, :]


def greet_ctx(barrier, me):
    def one(k, carry):
        pl.semaphore_signal(
            barrier, inc=1, device_id={"ctx": lax.rem(me + k, CTX)}, device_id_type=MESH
        )
        return carry

    lax.fori_loop(1, CTX, one, 0)


def prefix_kernel(
    key, value, prior, prior_total, rows, mine, inbox, outbox, got, send_a, recv_a, send_b, recv_b
):
    me = lax.axis_index("ctx")
    barrier = pltpu.get_barrier_semaphore()
    greet_ctx(barrier, me)
    states = []
    totals = []
    for b in range(2):
        features = phi(key[b * BLOCK : (b + 1) * BLOCK, :])
        states.append(dot_tn(features, value[b * BLOCK : (b + 1) * BLOCK, :]))
        totals.append(jnp.sum(features.astype(F32), axis=0, keepdims=True))
    rows[...] = states[0] + states[1]
    fill_parts(mine, rows, totals[0] + totals[1])
    pl.semaphore_wait(barrier, CTX - 1)
    spread_start(mine, inbox, send_a, recv_a, me)
    spread_wait(mine, inbox, send_a, recv_a, me)
    running(inbox, outbox, False)
    spread_start(outbox, got, send_b, recv_b, me)
    spread_wait(outbox, got, send_b, recv_b, me)
    join_parts(got, prior.at[0])
    prior[1] = prior[0] + states[0]
    before_total = got[0, PART : PART + 1, :]
    prior_total[0] = jnp.broadcast_to(before_total, (8, HEAD))
    prior_total[1] = jnp.broadcast_to(before_total + totals[0], (8, HEAD))


def exchange_scratch():
    return [
        pltpu.VMEM((HEAD, HEAD), F32),
        pltpu.VMEM((CTX, 2 * PART, HEAD), F32),
        pltpu.VMEM((CTX, 2 * PART, HEAD), F32),
        pltpu.VMEM((CTX, 2 * PART, HEAD), F32),
        pltpu.VMEM((CTX, 2 * PART, HEAD), F32),
        pltpu.SemaphoreType.DMA((CTX,)),
        pltpu.SemaphoreType.DMA((CTX,)),
        pltpu.SemaphoreType.DMA((CTX,)),
        pltpu.SemaphoreType.DMA((CTX,)),
    ]


def attention_kernel(
    query, cotangent, key, value, prior, prior_total, query_grad, gstate, gtotal, dkey, dvalue,
    features, sums, high, low,
):
    mask = lower_mask()

    @pl.when(pl.program_id(0) == 0)
    def _():
        triangle = jnp.where(mask, 1.0, 0.0).astype(BF16)
        for b in range(2):
            at = pl.ds(b * BLOCK, BLOCK)
            kf = phi(key[at, :])
            features[at, :] = kf
            sums[at, :] = dot_nn(triangle, kf) + prior_total[b, 0:1, :]
            high[b], low[b] = halves(prior[b])
        gstate[...] = jnp.zeros_like(gstate)
        gtotal[...] = jnp.zeros_like(gtotal)
        dkey[...] = jnp.zeros_like(dkey)
        dvalue[...] = jnp.zeros_like(dvalue)

    for b in range(2):
        at = pl.ds(b * BLOCK, BLOCK)
        raw = query[at, :]
        qf = phi(raw)
        wide = qf.astype(F32)
        kf = features[at, :]
        v = value[at, :]
        scores = jnp.where(mask, dot_nt(qf, kf), 0.0).astype(BF16)
        den = jnp.sum(wide * sums[at, :], axis=1, keepdims=True)
        numer = dot_nn(qf, high[b]) + dot_nn(qf, low[b]) + dot_nn(scores, v)
        inverse = 1.0 / den
        wide_cot = cotangent[at, :].astype(F32)
        g = (wide_cot * inverse).astype(BF16)
        c = -jnp.sum(wide_cot * numer, axis=1, keepdims=True) * inverse * inverse
        gstate[b] += dot_tn(qf, g)
        gtotal[b] += jnp.broadcast_to(jnp.sum(wide * c, axis=0, keepdims=True), (8, HEAD))
        dscores = jnp.where(mask, dot_nt(g, v) + c, 0.0).astype(BF16)
        dqf = (
            dot_nt(g, high[b])
            + dot_nt(g, low[b])
            + c * prior_total[b, 0:1, :]
            + dot_nn(dscores, kf)
        )
        query_grad[at, :] = (dqf * slope(raw)).astype(BF16)
        dkey[at, :] += dot_tn(dscores, qf)
        dvalue[at, :] += dot_tn(scores, g)


def remote(source, target, send, recv, device):
    return pltpu.make_async_remote_copy(
        src_ref=source,
        dst_ref=target,
        send_sem=send,
        recv_sem=recv,
        device_id=device,
        device_id_type=MESH,
    )


def weights_kernel(
    key, value, gstate, gtotal, dkey, dvalue, layer, key_out, value_out,
    rows, mine, inbox, outbox, got, send_a, recv_a, send_b, recv_b,
    turned, gathered, zsend, zrecv, reduced, arrived,
    y_send, y_recv, f_send, f_recv, z_send, z_recv, x_send, x_recv,
):
    me = lax.axis_index("ctx")
    head = lax.axis_index("head")
    x = me // ZS
    z = lax.rem(me, ZS)
    y = head // 2
    core = lax.rem(head, 2)
    sibling = {"head": head + 1 - 2 * core}
    y_peers = [None] + [
        {"head": lax.rem(y + away, YS) * 2 + core} for away in (YS - 1, 1, 2)
    ]
    z_peers = [
        {"ctx": x * ZS + lax.rem(z + 1, ZS)},
        {"ctx": x * ZS + lax.rem(z + ZS - 1, ZS)},
    ]
    barrier = pltpu.get_barrier_semaphore()
    greet_ctx(barrier, me)
    for device in y_peers[1:] + [sibling]:
        pl.semaphore_signal(barrier, inc=1, device_id=device, device_id_type=MESH)
    rows[...] = gstate[0] + gstate[1]
    fill_parts(mine, rows, gtotal[0, 0:1, :] + gtotal[1, 0:1, :])
    zsend_zero = jnp.zeros((HEAD, 2 * HEAD), BF16)
    for wave in range(YS):
        for way in range(2):
            zrecv[wave, way, 0] = zsend_zero
    pl.semaphore_wait(barrier, CTX - 1 + YS)
    spread_start(mine, inbox, send_a, recv_a, me)
    for j in range(8):
        block = layer[:, j * HEAD : (j + 1) * HEAD].T
        for q in range(4):
            at = ((j % 2) * 4 + q) * HEAD + (j // 2) * 32
            turned[at : at + 32, :] = block[q * 32 : (q + 1) * 32, :]
    spread_wait(mine, inbox, send_a, recv_a, me)
    running(inbox, outbox, True)
    spread_start(outbox, got, send_b, recv_b, me)
    spread_wait(outbox, got, send_b, recv_b, me)
    join_parts(got, rows)
    for b in (1, 0):
        at = pl.ds(b * BLOCK, BLOCK)
        later = rows[...]
        later_total = got[0, PART : PART + 1, :]
        if b == 0:
            later = later + gstate[1]
            later_total = later_total + gtotal[1, 0:1, :]
        high, low = halves(later)
        kf = phi(key[at, :])
        v = value[at, :]
        dk = dkey[at, :] + dot_nt(v, high) + dot_nt(v, low) + later_total
        gathered[0, core, at, 0:HEAD] = (dk * slope(key[at, :])).astype(BF16)
        dv = dvalue[at, :] + dot_nn(kf, high) + dot_nn(kf, low)
        gathered[0, core, at, HEAD : 2 * HEAD] = dv.astype(BF16)

    def forward(slot):
        return remote(
            gathered.at[slot, core],
            gathered.at[slot, core],
            f_send.at[slot],
            f_recv.at[slot],
            sibling,
        )

    def forward_in(slot):
        return remote(
            gathered.at[slot, 1 - core],
            gathered.at[slot, 1 - core],
            f_send.at[slot],
            f_recv.at[slot],
            sibling,
        )

    def across(slot):
        return remote(
            gathered.at[0, core],
            gathered.at[slot, core],
            y_send.at[slot],
            y_recv.at[slot],
            y_peers[slot],
        )

    forward(0).start()
    for slot in (1, 2, 3):
        across(slot).start()

    def hop(wave, way, step):
        return remote(
            zsend.at[wave, way, step],
            zrecv.at[wave, way, step + 1],
            z_send.at[wave, way, step],
            z_recv.at[wave, way, step + 1],
            z_peers[way],
        )

    def tick(t, carry):
        for wave in range(YS):
            step = t - wave

            @pl.when(step == 0)
            def _():
                forward_in(wave).wait_recv()

            @pl.when((step >= 0) & (step < ZS))
            def _():
                for way in range(2):
                    if way == 0:
                        to = lax.rem(z + 2 * ZS - 1 - step, ZS)
                    else:
                        to = lax.rem(z + 1 + step, ZS)
                    at = pl.ds(pl.multiple_of(to * HEAD, HEAD), HEAD)
                    local = dot_nn(turned[at, :], gathered[wave, way])

                    @pl.when(step > 0)
                    def _():
                        remote(
                            zsend.at[wave, way, step - 1],
                            zrecv.at[wave, way, step],
                            z_send.at[wave, way, step - 1],
                            z_recv.at[wave, way, step],
                            z_peers[way],
                        ).wait_recv()

                    both = local + zrecv[wave, way, step].astype(F32)
                    zsend[wave, way, step] = both.astype(BF16)

                    @pl.when(step < ZS - 1)
                    def _():
                        hop(wave, way, step).start()

                    @pl.when(step == ZS - 1)
                    def _():
                        reduced[wave, way] = both

            @pl.when(step == ZS - 1)
            def _():
                for k in range(1, XS):
                    x_copy(wave, k).start()

        for slot in range(1, YS):

            @pl.when(t == slot - 1)
            def _():
                across(slot).wait_recv()
                forward(slot).start()

        return carry

    def x_copy(wave, k):
        to = lax.rem(x + k, XS)
        at = pl.ds(pl.multiple_of(to * 32, 32), 32)
        return remote(
            zsend.at[wave, :, ZS - 1, at, :],
            arrived.at[wave, k - 1],
            x_send.at[wave, k],
            x_recv.at[wave, k],
            {"ctx": to * ZS + z},
        )

    lax.fori_loop(0, ZS + YS - 1, tick, 0)
    away = [0, 1, YS - 1, 2]
    for wave in range(YS):
        for k in range(1, XS):
            x_copy(wave, k).wait_recv()
        for way in range(2):
            mine_at = pl.ds(pl.multiple_of(x * 32, 32), 32)
            total = reduced[wave, way, mine_at, :]
            for k in range(1, XS):
                total = total + arrived[wave, k - 1, way].astype(F32)
            column = (lax.rem(y + away[wave], YS) * 2 + way) * HEAD
            column = pl.ds(pl.multiple_of(column, HEAD), HEAD)
            key_out[:, column] = total[:, 0:HEAD]
            value_out[:, column] = total[:, HEAD : 2 * HEAD]
    forward(0).wait_send()
    for slot in (1, 2, 3):
        across(slot).wait_send()
        forward(slot).wait_send()

    def drain(step, carry):
        for wave in range(YS):
            for way in range(2):
                hop(wave, way, step).wait_send()
        return carry

    lax.fori_loop(0, ZS - 1, drain, 0)
    for wave in range(YS):
        for k in range(1, XS):
            x_copy(wave, k).wait_send()


def shards(layer_input, query_columns, key_columns, value_columns, output_gradient):
    shape = jax.ShapeDtypeStruct
    prior, prior_total = pl.pallas_call(
        prefix_kernel,
        out_shape=(shape((2, HEAD, HEAD), F32), shape((2, 8, HEAD), F32)),
        in_specs=[VMEM] * 2,
        out_specs=(VMEM, VMEM),
        scratch_shapes=exchange_scratch(),
        compiler_params=pltpu.CompilerParams(collective_id=0, has_side_effects=True),
        name="prefix",
    )(key_columns, value_columns)

    def whole(*dims):
        return pl.BlockSpec(dims, lambda h: (0,) * len(dims))

    column = pl.BlockSpec((ROWS, HEAD), lambda h: (0, h))
    query_grad, gstate, gtotal, dkey, dvalue = pl.pallas_call(
        attention_kernel,
        out_shape=(
            shape((ROWS, GROUP * HEAD), BF16),
            shape((2, HEAD, HEAD), F32),
            shape((2, 8, HEAD), F32),
            shape((ROWS, HEAD), F32),
            shape((ROWS, HEAD), F32),
        ),
        grid=(GROUP,),
        in_specs=[
            column,
            column,
            whole(ROWS, HEAD),
            whole(ROWS, HEAD),
            whole(2, HEAD, HEAD),
            whole(2, 8, HEAD),
        ],
        out_specs=(
            column,
            whole(2, HEAD, HEAD),
            whole(2, 8, HEAD),
            whole(ROWS, HEAD),
            whole(ROWS, HEAD),
        ),
        scratch_shapes=[
            pltpu.VMEM((ROWS, HEAD), BF16),
            pltpu.VMEM((ROWS, HEAD), F32),
            pltpu.VMEM((2, HEAD, HEAD), BF16),
            pltpu.VMEM((2, HEAD, HEAD), BF16),
        ],
        compiler_params=pltpu.CompilerParams(
            dimension_semantics=("arbitrary",), vmem_limit_bytes=24 << 20
        ),
        name="attention",
    )(query_columns, output_gradient, key_columns, value_columns, prior, prior_total)

    sems = pltpu.SemaphoreType.DMA
    key_grad, value_grad = pl.pallas_call(
        weights_kernel,
        out_shape=(
            shape((32, KEY_VALUE_HEADS * HEAD), F32),
            shape((32, KEY_VALUE_HEADS * HEAD), F32),
        ),
        in_specs=[VMEM] * 7,
        out_specs=(VMEM, VMEM),
        scratch_shapes=exchange_scratch()
        + [
            pltpu.VMEM((GROUP * HEAD, ROWS), BF16),
            pltpu.VMEM((YS, 2, ROWS, 2 * HEAD), BF16),
            pltpu.VMEM((YS, 2, ZS, HEAD, 2 * HEAD), BF16),
            pltpu.VMEM((YS, 2, ZS, HEAD, 2 * HEAD), BF16),
            pltpu.VMEM((YS, 2, HEAD, 2 * HEAD), F32),
            pltpu.VMEM((YS, XS - 1, 2, 32, 2 * HEAD), BF16),
            sems((YS,)),
            sems((YS,)),
            sems((YS,)),
            sems((YS,)),
            sems((YS, 2, ZS)),
            sems((YS, 2, ZS)),
            sems((YS, XS)),
            sems((YS, XS)),
        ],
        compiler_params=pltpu.CompilerParams(
            collective_id=1, has_side_effects=True, vmem_limit_bytes=40 << 20
        ),
        name="weights",
    )(key_columns, value_columns, gstate, gtotal, dkey, dvalue, layer_input)
    return query_grad, key_grad, value_grad


def solution(mesh):
    placed = (P("ctx", "head"),) * 5
    return jax.shard_map(
        shards,
        mesh=mesh,
        in_specs=placed,
        out_specs=(P("ctx", "head"), P(("head", "ctx"), None), P(("head", "ctx"), None)),
        check_vma=False,
    )
```

```python
import jax
import jax.numpy as jnp
from jax import lax
from jax.experimental import pallas as pl
from jax.experimental.pallas import tpu as pltpu
from jax.sharding import PartitionSpec as P

QUERY_HEADS = 64
KEY_VALUE_HEADS = 8
GROUP = QUERY_HEADS // KEY_VALUE_HEADS
HEAD = 128
BLOCK = 256
ROWS = 512
XS = 4
ZS = 8
YS = 4
OUT = 32
MESSAGE = HEAD + 16
MESH = pl.DeviceIdType.MESH
F32 = jnp.float32
BF16 = jnp.bfloat16
HOPS = ((4, 3), (3, 4))
LAST = 4


def phi(raw):
    wide = raw.astype(F32)
    return jnp.where(wide > 0, wide + 1.0, jnp.exp(jnp.minimum(wide, 0.0))).astype(BF16)


def slope(raw):
    wide = raw.astype(F32)
    return jnp.where(wide > 0, 1.0, jnp.exp(jnp.minimum(wide, 0.0)))


def dot_nn(a, b):
    return lax.dot_general(a, b, (((1,), (0,)), ((), ())), preferred_element_type=F32)


def dot_nt(a, b):
    return lax.dot_general(a, b, (((1,), (1,)), ((), ())), preferred_element_type=F32)


def dot_tn(a, b):
    return lax.dot_general(a, b, (((0,), (0,)), ((), ())), preferred_element_type=F32)


def halves(value):
    high = value.astype(BF16)
    return high, (value - high.astype(F32)).astype(BF16)


def lower_mask():
    rows = lax.broadcasted_iota(jnp.int32, (BLOCK, BLOCK), 0)
    cols = lax.broadcasted_iota(jnp.int32, (BLOCK, BLOCK), 1)
    return cols <= rows


def remote(source, target, send, recv, device):
    return pltpu.make_async_remote_copy(
        src_ref=source,
        dst_ref=target,
        send_sem=send,
        recv_sem=recv,
        device_id=device,
        device_id_type=MESH,
    )


def pack(target, state, total):
    target[0:HEAD, :] = state.astype(BF16)
    high, low = halves(total)
    row = lax.broadcasted_iota(jnp.int32, (16, HEAD), 0)
    tail = jnp.where(row == 0, high.astype(F32), jnp.where(row == 1, low.astype(F32), 0.0))
    target[HEAD:MESSAGE, :] = tail.astype(BF16)


def parts(message):
    return message[0:HEAD, :], message[HEAD : HEAD + 1, :] + message[HEAD + 1 : HEAD + 2, :]


def kernel(
    query_hbm, cotangent_hbm, key_hbm, value_hbm, layer_hbm,
    query_grad_hbm, key_out, value_out,
    query, cotangent, key, value, layer,
    features, sums, states, totals, high, low, prior_total, rowsum,
    qf_all, scores_all, numer_all, g_all, c_all, grad_all,
    gstate, gtotal, dkey, dvalue,
    message, from_z, from_x,
    turned, gathered, zsend, zrecv, reduced, reduced_low, arrived,
    load, zs, zr, xs, xr, y_send, y_recv, f_send, f_recv, p_send, p_recv, x_send, x_recv,
):
    me = lax.axis_index("ctx")
    head = lax.axis_index("head")
    x = me // ZS
    z = lax.rem(me, ZS)
    y = head // 2
    core = lax.rem(head, 2)
    sibling = {"head": head + 1 - 2 * core}
    z_line = [{"ctx": x * ZS + lax.rem(z + k, ZS)} for k in range(ZS)]
    x_line = [{"ctx": lax.rem(x + k, XS) * ZS + z} for k in range(XS)]
    y_line = [{"head": lax.rem(y + k, YS) * 2 + core} for k in (0, YS - 1, 1, 2)]
    away = (0, 1, YS - 1, 2)

    loads = [
        pltpu.make_async_copy(source, target, load.at[i])
        for i, (source, target) in enumerate(
            (
                (key_hbm, key),
                (value_hbm, value),
                (query_hbm, query),
                (cotangent_hbm, cotangent),
                (layer_hbm, layer),
            )
        )
    ]
    for copy in loads:
        copy.start()
    barrier = pltpu.get_barrier_semaphore()
    for device in z_line[1:] + x_line[1:] + y_line[1:] + [sibling]:
        pl.semaphore_signal(barrier, inc=1, device_id=device, device_id_type=MESH)

    def z_copy(e, k):
        return remote(message.at[e, 0], from_z.at[e, k], zs.at[e, k], zr.at[e, k], z_line[k])

    def x_copy(e, k):
        return remote(message.at[e, 1], from_x.at[e, k], xs.at[e, k], xr.at[e, k], x_line[k])

    def z_finish(e, state, total, reverse):
        line_state, line_total = state, total
        part_state, part_total = jnp.zeros_like(state), jnp.zeros_like(total)
        for k in range(1, ZS):
            z_copy(e, k).wait_recv()
            got_state, got_total = parts(from_z[e, k].astype(F32))
            line_state, line_total = line_state + got_state, line_total + got_total
            counts = (k > z) if reverse else (k <= z)
            part_state = part_state + jnp.where(counts, got_state, 0.0)
            part_total = part_total + jnp.where(counts, got_total, 0.0)
        pack(message.at[e, 1], line_state, line_total)
        for k in range(1, XS):
            x_copy(e, k).start()
        rowsum[0:HEAD, :] = part_state
        rowsum[HEAD : HEAD + 8, :] = jnp.broadcast_to(part_total, (8, HEAD))

    def x_finish(e, reverse):
        state, total = rowsum[0:HEAD, :], rowsum[HEAD : HEAD + 1, :]
        for k in range(1, XS):
            x_copy(e, k).wait_recv()
            got_state, got_total = parts(from_x[e, k].astype(F32))
            counts = (k > x) if reverse else (k <= x)
            state = state + jnp.where(counts, got_state, 0.0)
            total = total + jnp.where(counts, got_total, 0.0)
        return state, total

    mask = lower_mask()
    blocks = [pl.ds(b * BLOCK, BLOCK) for b in range(2)]

    loads[0].wait()
    loads[1].wait()
    for b in range(2):
        kf = phi(key[blocks[b], :])
        features[blocks[b], :] = kf
        states[b] = dot_tn(kf, value[blocks[b], :])
        totals[b] = jnp.broadcast_to(
            jnp.sum(kf.astype(F32), axis=0, keepdims=True), (8, HEAD)
        )
    own_total = totals[0, 0:1, :] + totals[1, 0:1, :]
    pack(message.at[0, 0], states[0] + states[1], own_total)
    pl.semaphore_wait(barrier, ZS - 1 + XS - 1 + YS - 1 + 1)
    for k in range(1, ZS):
        z_copy(0, k).start()

    triangle = jnp.where(mask, 1.0, 0.0).astype(BF16)
    for b in range(2):
        sums[blocks[b], :] = dot_nn(triangle, features[blocks[b], :])
    zero = jnp.zeros((HEAD, 2 * HEAD), BF16)
    for wave in range(YS):
        for way in range(2):
            for side in range(2):
                zrecv[wave, way, side, 0] = zero
    gstate[...] = jnp.zeros_like(gstate)
    gtotal[...] = jnp.zeros_like(gtotal)
    dkey[...] = jnp.zeros_like(dkey)
    dvalue[...] = jnp.zeros_like(dvalue)

    def columns(h):
        return pl.ds(pl.multiple_of(h * HEAD, HEAD), HEAD)

    def inside(h, carry):
        at = columns(h)
        for b in range(2):
            qf = phi(query[blocks[b], at])
            qf_all[blocks[b], at] = qf
            scores = jnp.where(mask, dot_nt(qf, features[blocks[b], :]), 0.0).astype(BF16)
            scores_all[h, b] = scores
            numer_all[blocks[b], at] = dot_nn(scores, value[blocks[b], :])
        return carry

    def forward_pass(h, carry):
        at = columns(h)
        for b in range(2):
            qf = qf_all[blocks[b], at]
            wide = qf.astype(F32)
            den = jnp.sum(wide * sums[blocks[b], :], axis=1, keepdims=True)
            numer = numer_all[blocks[b], at] + dot_nn(qf, high[b]) + dot_nn(qf, low[b])
            inverse = 1.0 / den
            wide_cot = cotangent[blocks[b], at].astype(F32)
            g = (wide_cot * inverse).astype(BF16)
            c = -jnp.sum(wide_cot * numer, axis=1, keepdims=True) * inverse * inverse
            c = jnp.broadcast_to(c, (BLOCK, HEAD))
            g_all[blocks[b], at] = g
            c_all[blocks[b], at] = c
            gstate[b] += dot_tn(qf, g)
            gtotal[b] += jnp.broadcast_to(jnp.sum(wide * c, axis=0, keepdims=True), (8, HEAD))
        return carry

    def backward_pass(h, carry):
        at = columns(h)
        for b in range(2):
            g = g_all[blocks[b], at]
            qf = qf_all[blocks[b], at]
            c = c_all[blocks[b], at]
            kf = features[blocks[b], :]
            dscores = dot_nt(g, value[blocks[b], :]) + jnp.concatenate([c, c], axis=1)
            dscores = jnp.where(mask, dscores, 0.0).astype(BF16)
            dqf = (
                dot_nt(g, high[b])
                + dot_nt(g, low[b])
                + c * prior_total[b, 0:1, :]
                + dot_nn(dscores, kf)
            )
            grad_all[blocks[b], at] = (dqf * slope(query[blocks[b], at])).astype(BF16)
            dkey[blocks[b], :] += dot_tn(dscores, qf)
            dvalue[blocks[b], :] += dot_tn(scores_all[h, b], g)
        return carry

    loads[2].wait()
    lax.fori_loop(0, GROUP // 2, inside, 0)
    z_finish(0, states[0] + states[1], own_total, False)
    lax.fori_loop(GROUP // 2, GROUP, inside, 0)
    loads[3].wait()
    state, total = x_finish(0, False)
    for b in range(2):
        high[b], low[b] = halves(state)
        prior_total[b] = jnp.broadcast_to(total, (8, HEAD))
        sums[blocks[b], :] += total
        state = state + states[b]
        total = total + totals[b, 0:1, :]
    lax.fori_loop(0, GROUP, forward_pass, 0)
    own_gtotal = gtotal[0, 0:1, :] + gtotal[1, 0:1, :]
    pack(message.at[1, 0], gstate[0] + gstate[1], own_gtotal)
    for k in range(1, ZS):
        z_copy(1, k).start()
    lax.fori_loop(0, GROUP // 2, backward_pass, 0)
    z_finish(1, gstate[0] + gstate[1], own_gtotal, True)
    lax.fori_loop(GROUP // 2, GROUP, backward_pass, 0)
    grad_copy = pltpu.make_async_copy(grad_all, query_grad_hbm, load.at[5])
    grad_copy.start()
    loads[4].wait()
    for j in range(8):
        block = layer[:, j * HEAD : (j + 1) * HEAD].T
        for q in range(4):
            turned[(j % 2) * 4 + q, j // 2] = block[q * OUT : (q + 1) * OUT, :]
    later, later_total = x_finish(1, True)
    for b in (1, 0):
        later_high, later_low = halves(later)
        v = value[blocks[b], :]
        kf = features[blocks[b], :]
        dk = dkey[blocks[b], :] + dot_nt(v, later_high) + dot_nt(v, later_low) + later_total
        gathered[0, core, blocks[b], 0:HEAD] = (dk * slope(key[blocks[b], :])).astype(BF16)
        dv = dvalue[blocks[b], :] + dot_nn(kf, later_high) + dot_nn(kf, later_low)
        gathered[0, core, blocks[b], HEAD : 2 * HEAD] = dv.astype(BF16)
        later = later + gstate[b]
        later_total = later_total + gtotal[b, 0:1, :]

    def forward(slot):
        return remote(
            gathered.at[slot, core],
            gathered.at[slot, core],
            f_send.at[slot],
            f_recv.at[slot],
            sibling,
        )

    def forward_in(slot):
        return remote(
            gathered.at[slot, 1 - core],
            gathered.at[slot, 1 - core],
            f_send.at[slot],
            f_recv.at[slot],
            sibling,
        )

    def across(slot):
        return remote(
            gathered.at[0, core],
            gathered.at[slot, core],
            y_send.at[slot],
            y_recv.at[slot],
            y_line[slot],
        )

    forward(0).start()
    for slot in (1, 2, 3):
        across(slot).start()

    def hop(wave, way, side, step):
        return remote(
            zsend.at[wave, way, side, step],
            zrecv.at[wave, way, side, step + 1],
            p_send.at[wave, way, side, step],
            p_recv.at[wave, way, side, step + 1],
            z_line[1 if side == 0 else ZS - 1],
        )

    def owed(wave, k):
        to = lax.rem(x + k, XS)
        at = pl.ds(pl.multiple_of(to * OUT, OUT), OUT)
        return remote(
            reduced_low.at[wave, :, at, :],
            arrived.at[wave, k],
            x_send.at[wave, k],
            x_recv.at[wave, k],
            x_line[k],
        )

    def local(wave, way, to):
        rows = turned[to].reshape(HEAD, ROWS)
        return dot_nn(rows, gathered[wave, way])

    def tick(i, carry):
        wave = lax.rem(i, YS)
        step = i // YS - wave

        for slot in range(1, YS):

            @pl.when((step == -1) & (wave == slot))
            def _():
                across(slot).wait_recv()
                forward(slot).start()

        @pl.when(step == 0)
        def _():
            forward_in(wave).wait_recv()

        for way in range(2):
            for side in range(2):
                hops = HOPS[way][side]

                @pl.when((step >= 0) & (step < hops))
                def _():
                    left = hops - step
                    to = lax.rem(z + left, ZS) if side == 0 else lax.rem(z + ZS - left, ZS)
                    mine = local(wave, way, to)

                    @pl.when(step > 0)
                    def _():
                        hop(wave, way, side, step - 1).wait_recv()

                    both = mine + zrecv[wave, way, side, step].astype(F32)
                    zsend[wave, way, side, step] = both.astype(BF16)
                    hop(wave, way, side, step).start()

        @pl.when(step == LAST)
        def _():
            for way in range(2):
                total = local(wave, way, z)
                for side in range(2):
                    hops = HOPS[way][side]
                    hop(wave, way, side, hops - 1).wait_recv()
                    total = total + zrecv[wave, way, side, hops].astype(F32)
                reduced[wave, way] = total
                reduced_low[wave, way] = total.astype(BF16)
            for k in range(1, XS):
                owed(wave, k).start()

        return carry

    lax.fori_loop(0, YS * (LAST + YS), tick, 0)
    mine_at = pl.ds(pl.multiple_of(x * OUT, OUT), OUT)
    for wave in range(YS):
        for k in range(1, XS):
            owed(wave, k).wait_recv()
        for way in range(2):
            total = reduced[wave, way, mine_at, :]
            for k in range(1, XS):
                total = total + arrived[wave, k, way].astype(F32)
            column = columns(lax.rem(y + away[wave], YS) * 2 + way)
            key_out[:, column] = total[:, 0:HEAD]
            value_out[:, column] = total[:, HEAD : 2 * HEAD]

    for e in range(2):
        for k in range(1, ZS):
            z_copy(e, k).wait_send()
        for k in range(1, XS):
            x_copy(e, k).wait_send()
    forward(0).wait_send()
    for slot in (1, 2, 3):
        across(slot).wait_send()
        forward(slot).wait_send()

    def drain(wave, carry):
        for way in range(2):
            for side in range(2):
                for step in range(HOPS[way][side]):
                    hop(wave, way, side, step).wait_send()
        for k in range(1, XS):
            owed(wave, k).wait_send()
        return carry

    lax.fori_loop(0, YS, drain, 0)
    grad_copy.wait()


def shards(layer_input, query_columns, key_columns, value_columns, output_gradient):
    shape = jax.ShapeDtypeStruct
    vmem = pltpu.VMEM
    sems = pltpu.SemaphoreType.DMA
    wide = GROUP * HEAD
    far = pl.BlockSpec(memory_space=pl.ANY)
    near = pl.BlockSpec(memory_space=pltpu.VMEM)
    return pl.pallas_call(
        kernel,
        out_shape=(
            shape((ROWS, wide), BF16),
            shape((OUT, KEY_VALUE_HEADS * HEAD), F32),
            shape((OUT, KEY_VALUE_HEADS * HEAD), F32),
        ),
        in_specs=[far] * 5,
        out_specs=(far, near, near),
        scratch_shapes=[
            vmem((ROWS, wide), BF16),
            vmem((ROWS, wide), BF16),
            vmem((ROWS, HEAD), BF16),
            vmem((ROWS, HEAD), BF16),
            vmem((ROWS, wide), BF16),
            vmem((ROWS, HEAD), BF16),
            vmem((ROWS, HEAD), F32),
            vmem((2, HEAD, HEAD), F32),
            vmem((2, 8, HEAD), F32),
            vmem((2, HEAD, HEAD), BF16),
            vmem((2, HEAD, HEAD), BF16),
            vmem((2, 8, HEAD), F32),
            vmem((HEAD + 8, HEAD), F32),
            vmem((ROWS, wide), BF16),
            vmem((GROUP, 2, BLOCK, BLOCK), BF16),
            vmem((ROWS, wide), F32),
            vmem((ROWS, wide), BF16),
            vmem((ROWS, wide), F32),
            vmem((ROWS, wide), BF16),
            vmem((2, HEAD, HEAD), F32),
            vmem((2, 8, HEAD), F32),
            vmem((ROWS, HEAD), F32),
            vmem((ROWS, HEAD), F32),
            vmem((2, 2, MESSAGE, HEAD), BF16),
            vmem((2, ZS, MESSAGE, HEAD), BF16),
            vmem((2, XS, MESSAGE, HEAD), BF16),
            vmem((ZS, XS, OUT, ROWS), BF16),
            vmem((YS, 2, ROWS, 2 * HEAD), BF16),
            vmem((YS, 2, 2, LAST, HEAD, 2 * HEAD), BF16),
            vmem((YS, 2, 2, LAST + 1, HEAD, 2 * HEAD), BF16),
            vmem((YS, 2, HEAD, 2 * HEAD), F32),
            vmem((YS, 2, HEAD, 2 * HEAD), BF16),
            vmem((YS, XS, 2, OUT, 2 * HEAD), BF16),
            sems((6,)),
            sems((2, ZS)),
            sems((2, ZS)),
            sems((2, XS)),
            sems((2, XS)),
            sems((YS,)),
            sems((YS,)),
            sems((YS,)),
            sems((YS,)),
            sems((YS, 2, 2, LAST)),
            sems((YS, 2, 2, LAST + 1)),
            sems((YS, XS)),
            sems((YS, XS)),
        ],
        compiler_params=pltpu.CompilerParams(
            collective_id=0, has_side_effects=True, vmem_limit_bytes=48 << 20
        ),
        name="backward",
    )(query_columns, output_gradient, key_columns, value_columns, layer_input)


def solution(mesh):
    placed = (P("ctx", "head"),) * 5
    return jax.shard_map(
        shards,
        mesh=mesh,
        in_specs=placed,
        out_specs=(P("ctx", "head"), P(("head", "ctx"), None), P(("head", "ctx"), None)),
        check_vma=False,
    )
```

```python
import jax
import jax.numpy as jnp
from jax import lax
from jax.experimental import pallas as pl
from jax.experimental.pallas import tpu as pltpu
from jax.sharding import PartitionSpec as P

QUERY_HEADS = 64
KEY_VALUE_HEADS = 8
GROUP = QUERY_HEADS // KEY_VALUE_HEADS
HEAD = 128
BLOCK = 256
ROWS = 512
XS = 4
ZS = 8
YS = 4
OUT = 32
MESSAGE = HEAD + 16
MESH = pl.DeviceIdType.MESH
F32 = jnp.float32
BF16 = jnp.bfloat16
HALF = 512
LONG = 4
SHORT = 3
ZFIRST = 3
XFIRST = 5
LIMIT = 60 << 20


def phi(raw):
    wide = raw.astype(F32)
    return jnp.where(wide > 0, wide + 1.0, jnp.exp(jnp.minimum(wide, 0.0))).astype(BF16)


def slope(raw):
    wide = raw.astype(F32)
    return jnp.where(wide > 0, 1.0, jnp.exp(jnp.minimum(wide, 0.0)))


def dot_nn(a, b):
    return lax.dot_general(a, b, (((1,), (0,)), ((), ())), preferred_element_type=F32)


def dot_nt(a, b):
    return lax.dot_general(a, b, (((1,), (1,)), ((), ())), preferred_element_type=F32)


def dot_tn(a, b):
    return lax.dot_general(a, b, (((0,), (0,)), ((), ())), preferred_element_type=F32)


def halves(value):
    high = value.astype(BF16)
    return high, (value - high.astype(F32)).astype(BF16)


def lower_mask():
    rows = lax.broadcasted_iota(jnp.int32, (BLOCK, BLOCK), 0)
    cols = lax.broadcasted_iota(jnp.int32, (BLOCK, BLOCK), 1)
    return cols <= rows


def remote(source, target, send, recv, device):
    return pltpu.make_async_remote_copy(
        src_ref=source,
        dst_ref=target,
        send_sem=send,
        recv_sem=recv,
        device_id=device,
        device_id_type=MESH,
    )


def pack(target, state, total):
    target[0:HEAD, :] = state.astype(BF16)
    high, low = halves(total)
    row = lax.broadcasted_iota(jnp.int32, (16, HEAD), 0)
    tail = jnp.where(row == 0, high.astype(F32), jnp.where(row == 1, low.astype(F32), 0.0))
    target[HEAD:MESSAGE, :] = tail.astype(BF16)


def parts(message):
    return message[0:HEAD, :], message[HEAD : HEAD + 1, :] + message[HEAD + 1 : HEAD + 2, :]


def kernel(
    query_hbm, cotangent_hbm, key_hbm, value_hbm, layer_hbm,
    query_grad_hbm, key_out, value_out,
    query, cotangent, key, value, layer,
    features, sums, states, totals, high, low, prior_total, rowsum,
    qf_all, scores_all, numer_all, g_all, c_all, grad_all,
    gstate, gtotal, dkey, dvalue,
    message, from_z, from_x,
    turned, paired, zsend, zrecv, xsend, xrecv, x_owed, z_owed, x_arrived, z_arrived,
    load, zs, zr, xs, xr, l_send, l_recv, f_send, f_recv,
    p_send, p_recv, q_send, q_recv, x_send, x_recv, z_send, z_recv,
):
    me = lax.axis_index("ctx")
    head = lax.axis_index("head")
    x = me // ZS
    z = lax.rem(me, ZS)
    y = head // 2
    core = lax.rem(head, 2)
    sibling = {"head": head + 1 - 2 * core}
    z_line = [{"ctx": x * ZS + lax.rem(z + k, ZS)} for k in range(ZS)]
    x_line = [{"ctx": lax.rem(x + k, XS) * ZS + z} for k in range(XS)]
    y_line = [{"head": lax.rem(y + k, YS) * 2 + core} for k in range(YS)]

    loads = [
        pltpu.make_async_copy(source, target, load.at[i])
        for i, (source, target) in enumerate(
            (
                (key_hbm, key),
                (value_hbm, value),
                (query_hbm, query),
                (cotangent_hbm, cotangent),
                (layer_hbm, layer.at[0]),
            )
        )
    ]
    for copy in loads:
        copy.start()
    barrier = pltpu.get_barrier_semaphore()
    for device in z_line[1:] + x_line[1:] + y_line[1:] + [sibling]:
        pl.semaphore_signal(barrier, inc=1, device_id=device, device_id_type=MESH)

    def z_copy(e, k):
        return remote(message.at[e, 0], from_z.at[e, k], zs.at[e, k], zr.at[e, k], z_line[k])

    def x_copy(e, k):
        return remote(message.at[e, 1], from_x.at[e, k], xs.at[e, k], xr.at[e, k], x_line[k])

    def z_finish(e, state, total, reverse):
        line_state, line_total = state, total
        part_state, part_total = jnp.zeros_like(state), jnp.zeros_like(total)
        for k in range(1, ZS):
            z_copy(e, k).wait_recv()
            got_state, got_total = parts(from_z[e, k].astype(F32))
            line_state, line_total = line_state + got_state, line_total + got_total
            counts = (k > z) if reverse else (k <= z)
            part_state = part_state + jnp.where(counts, got_state, 0.0)
            part_total = part_total + jnp.where(counts, got_total, 0.0)
        pack(message.at[e, 1], line_state, line_total)
        for k in range(1, XS):
            x_copy(e, k).start()
        rowsum[0:HEAD, :] = part_state
        rowsum[HEAD : HEAD + 8, :] = jnp.broadcast_to(part_total, (8, HEAD))

    def x_finish(e, reverse):
        state, total = rowsum[0:HEAD, :], rowsum[HEAD : HEAD + 1, :]
        for k in range(1, XS):
            x_copy(e, k).wait_recv()
            got_state, got_total = parts(from_x[e, k].astype(F32))
            counts = (k > x) if reverse else (k <= x)
            state = state + jnp.where(counts, got_state, 0.0)
            total = total + jnp.where(counts, got_total, 0.0)
        return state, total

    mask = lower_mask()
    blocks = [pl.ds(b * BLOCK, BLOCK) for b in range(2)]

    loads[0].wait()
    loads[1].wait()
    for b in range(2):
        kf = phi(key[blocks[b], :])
        features[blocks[b], :] = kf
        states[b] = dot_tn(kf, value[blocks[b], :])
        totals[b] = jnp.broadcast_to(
            jnp.sum(kf.astype(F32), axis=0, keepdims=True), (8, HEAD)
        )
    own_total = totals[0, 0:1, :] + totals[1, 0:1, :]
    pack(message.at[0, 0], states[0] + states[1], own_total)
    pl.semaphore_wait(barrier, ZS - 1 + XS - 1 + YS - 1 + 1)
    for k in range(1, ZS):
        z_copy(0, k).start()

    def layer_copy(slot, half):
        part = pl.ds(half * HALF, HALF)
        return remote(
            layer.at[0, :, part],
            layer.at[slot, :, part],
            l_send.at[slot, half],
            l_recv.at[slot, half],
            y_line[YS - 1 if slot == 1 else 1],
        )

    def layer_relay(half):
        part = pl.ds(half * HALF, HALF)
        return remote(
            layer.at[1 + core, :, part],
            layer.at[3, :, part],
            l_send.at[3, half],
            l_recv.at[3, half],
            {"head": lax.rem(y + YS - 1 + 2 * core, YS) * 2 + core},
        )

    def turn(slot, half):
        def one(i, carry):
            j = half * 4 + i
            block = layer[slot, :, pl.ds(pl.multiple_of(j * HEAD, HEAD), HEAD)].T
            for q in range(4):
                turned[slot, lax.rem(j, 2) * 4 + q, j // 2] = block[q * OUT : (q + 1) * OUT, :]
            return carry

        lax.fori_loop(0, 4, one, 0)

    loads[4].wait()
    for slot in (1, 2):
        layer_copy(slot, 0).start()

    triangle = jnp.where(mask, 1.0, 0.0).astype(BF16)
    for b in range(2):
        sums[blocks[b], :] = dot_nn(triangle, features[blocks[b], :])
    zero = jnp.zeros((HEAD, 2 * HEAD), BF16)
    for v in range(ZFIRST):
        for side in range(2):
            zrecv[v, side, 0] = zero
    gstate[...] = jnp.zeros_like(gstate)
    gtotal[...] = jnp.zeros_like(gtotal)
    dkey[...] = jnp.zeros_like(dkey)
    dvalue[...] = jnp.zeros_like(dvalue)

    def columns(h):
        return pl.ds(pl.multiple_of(h * HEAD, HEAD), HEAD)

    def inside(h, carry):
        at = columns(h)
        for b in range(2):
            qf = phi(query[blocks[b], at])
            qf_all[blocks[b], at] = qf
            scores = jnp.where(mask, dot_nt(qf, features[blocks[b], :]), 0.0).astype(BF16)
            scores_all[h, b] = scores
            numer_all[blocks[b], at] = dot_nn(scores, value[blocks[b], :])
        return carry

    def forward_pass(h, carry):
        at = columns(h)
        for b in range(2):
            qf = qf_all[blocks[b], at]
            wide = qf.astype(F32)
            den = jnp.sum(wide * sums[blocks[b], :], axis=1, keepdims=True)
            numer = numer_all[blocks[b], at] + dot_nn(qf, high[b]) + dot_nn(qf, low[b])
            inverse = 1.0 / den
            wide_cot = cotangent[blocks[b], at].astype(F32)
            g = (wide_cot * inverse).astype(BF16)
            c = -jnp.sum(wide_cot * numer, axis=1, keepdims=True) * inverse * inverse
            c = jnp.broadcast_to(c, (BLOCK, HEAD))
            g_all[blocks[b], at] = g
            c_all[blocks[b], at] = c
            gstate[b] += dot_tn(qf, g)
            gtotal[b] += jnp.broadcast_to(jnp.sum(wide * c, axis=0, keepdims=True), (8, HEAD))
        return carry

    def backward_pass(h, carry):
        at = columns(h)
        for b in range(2):
            g = g_all[blocks[b], at]
            qf = qf_all[blocks[b], at]
            c = c_all[blocks[b], at]
            kf = features[blocks[b], :]
            dscores = dot_nt(g, value[blocks[b], :]) + jnp.concatenate([c, c], axis=1)
            dscores = jnp.where(mask, dscores, 0.0).astype(BF16)
            dqf = (
                dot_nt(g, high[b])
                + dot_nt(g, low[b])
                + c * prior_total[b, 0:1, :]
                + dot_nn(dscores, kf)
            )
            grad_all[blocks[b], at] = (dqf * slope(query[blocks[b], at])).astype(BF16)
            dkey[blocks[b], :] += dot_tn(dscores, qf)
            dvalue[blocks[b], :] += dot_tn(scores_all[h, b], g)
        return carry

    loads[2].wait()
    lax.fori_loop(0, GROUP // 2, inside, 0)
    z_finish(0, states[0] + states[1], own_total, False)
    for slot in (1, 2):
        layer_copy(slot, 1).start()
    lax.fori_loop(GROUP // 2, GROUP, inside, 0)
    turn(0, 0)
    turn(0, 1)
    loads[3].wait()
    state, total = x_finish(0, False)
    for b in range(2):
        high[b], low[b] = halves(state)
        prior_total[b] = jnp.broadcast_to(total, (8, HEAD))
        sums[blocks[b], :] += total
        state = state + states[b]
        total = total + totals[b, 0:1, :]
    lax.fori_loop(0, GROUP, forward_pass, 0)
    own_gtotal = gtotal[0, 0:1, :] + gtotal[1, 0:1, :]
    pack(message.at[1, 0], gstate[0] + gstate[1], own_gtotal)
    for k in range(1, ZS):
        z_copy(1, k).start()
    for slot in (1, 2):
        layer_copy(slot, 0).wait_recv()
    layer_relay(0).start()
    lax.fori_loop(0, GROUP // 2, backward_pass, 0)
    turn(1, 0)
    turn(2, 0)
    z_finish(1, gstate[0] + gstate[1], own_gtotal, True)
    lax.fori_loop(GROUP // 2, GROUP, backward_pass, 0)
    grad_copy = pltpu.make_async_copy(grad_all, query_grad_hbm, load.at[5])
    grad_copy.start()
    for slot in (1, 2):
        layer_copy(slot, 1).wait_recv()
    layer_relay(1).start()
    later, later_total = x_finish(1, True)
    for b in (1, 0):
        later_high, later_low = halves(later)
        v = value[blocks[b], :]
        kf = features[blocks[b], :]
        dk = dkey[blocks[b], :] + dot_nt(v, later_high) + dot_nt(v, later_low) + later_total
        paired[core, blocks[b], 0:HEAD] = (dk * slope(key[blocks[b], :])).astype(BF16)
        dv = dvalue[blocks[b], :] + dot_nn(kf, later_high) + dot_nn(kf, later_low)
        paired[core, blocks[b], HEAD : 2 * HEAD] = dv.astype(BF16)
        later = later + gstate[b]
        later_total = later_total + gtotal[b, 0:1, :]

    swap = remote(paired.at[core], paired.at[core], f_send.at[0], f_recv.at[0], sibling)
    swap_in = remote(paired.at[1 - core], paired.at[1 - core], f_send.at[0], f_recv.at[0], sibling)
    swap.start()
    swap_in.wait_recv()

    def away_of(slot):
        return slot + (slot // 2) * (1 - 2 * lax.rem(slot, 2))

    def z_local(slot, way, to):
        return dot_nn(turned[slot, to].reshape(XS * OUT, ROWS), paired[way])

    def x_local(slot, way, to):
        return dot_nn(turned[slot, :, to].reshape(ZS * OUT, ROWS), paired[way])

    def z_hop(v, side, step):
        sign = (1 - 2 * lax.rem(v, 2)) * (1 - 2 * side)
        return remote(
            zsend.at[v, side, step],
            zrecv.at[v, side, step + 1],
            p_send.at[v, side, step],
            p_recv.at[v, side, step + 1],
            {"ctx": x * ZS + lax.rem(z + ZS + sign, ZS)},
        )

    def x_hop(u, kind):
        sign = 1 - 2 * lax.rem(u, 2)
        if kind == 2:
            sign = -sign
        return remote(
            xsend.at[u, kind],
            xrecv.at[u, kind],
            q_send.at[u, kind],
            q_recv.at[u, kind],
            {"ctx": lax.rem(x + XS + sign, XS) * ZS + z},
        )

    def x_owe(v, k):
        to = lax.rem(x + k, XS)
        return remote(
            x_owed.at[v, to],
            x_arrived.at[v, k],
            x_send.at[v, k],
            x_recv.at[v, k],
            {"ctx": to * ZS + z, "head": lax.rem(y + away_of(v), YS) * 2 + core},
        )

    def z_owe(u, slot, k):
        to = lax.rem(z + k, ZS)
        return remote(
            z_owed.at[u, to],
            z_arrived.at[u, k],
            z_send.at[u, k],
            z_recv.at[u, k],
            {"ctx": x * ZS + to, "head": lax.rem(y + away_of(slot), YS) * 2 + core},
        )

    def z_first(v, step):
        for side, hops in ((0, LONG), (1, SHORT)):

            @pl.when((step >= 0) & (step < hops))
            def _():
                sign = (1 - 2 * lax.rem(v, 2)) * (1 - 2 * side)
                to = lax.rem(z + ZS + sign * (hops - step), ZS)
                mine = z_local(v, 0, to)

                @pl.when(step > 0)
                def _():
                    z_hop(v, side, step - 1).wait_recv()

                both = mine + zrecv[v, side, step].astype(F32)
                zsend[v, side, step] = both.astype(BF16)
                z_hop(v, side, step).start()

        @pl.when(step == LONG)
        def _():
            total = z_local(v, 0, z)
            z_hop(v, 0, LONG - 1).wait_recv()
            z_hop(v, 1, SHORT - 1).wait_recv()
            total = total + zrecv[v, 0, LONG].astype(F32) + zrecv[v, 1, SHORT].astype(F32)
            x_owed[v] = total.astype(BF16).reshape(XS, OUT, 2 * HEAD)
            for k in range(1, XS):
                x_owe(v, k).start()

            @pl.when(v == 0)
            def _():
                x_arrived[0, 0] = x_owed[0, x]

            @pl.when(v > 0)
            def _():
                x_owe(v, 0).start()

    def x_first(u, slot, way, step):
        sign = 1 - 2 * lax.rem(u, 2)

        @pl.when(step == 0)
        def _():
            xsend[u, 0] = x_local(slot, way, lax.rem(x + 2, XS)).astype(BF16)
            x_hop(u, 0).start()
            xsend[u, 2] = x_local(slot, way, lax.rem(x + XS - sign, XS)).astype(BF16)
            x_hop(u, 2).start()

        @pl.when(step == 1)
        def _():
            mine = x_local(slot, way, lax.rem(x + XS + sign, XS))
            x_hop(u, 0).wait_recv()
            xsend[u, 1] = (mine + xrecv[u, 0].astype(F32)).astype(BF16)
            x_hop(u, 1).start()

        @pl.when(step == 2)
        def _():
            total = x_local(slot, way, x)
            x_hop(u, 1).wait_recv()
            x_hop(u, 2).wait_recv()
            total = total + xrecv[u, 1].astype(F32) + xrecv[u, 2].astype(F32)
            z_owed[u] = total.astype(BF16).reshape(ZS, OUT, 2 * HEAD)

            def one(k, carry):
                z_owe(u, slot, k).start()
                return carry

            lax.fori_loop(1, ZS, one, 0)

            @pl.when(slot == 0)
            def _():
                z_arrived[0, 0] = z_owed[0, z]

            @pl.when(slot > 0)
            def _():
                z_owe(u, slot, 0).start()

    def tick(i, carry):
        slot = lax.rem(i, YS)
        step = i // YS - slot

        @pl.when((step == 0) & ((slot == 1) | (slot == 2)))
        def _():
            turn(slot, 1)

        @pl.when((step == 0) & (slot == 3))
        def _():
            layer_relay(0).wait_recv()
            turn(3, 0)
            layer_relay(1).wait_recv()
            turn(3, 1)

        x_first(slot, slot, 1, step)

        @pl.when(slot < ZFIRST)
        def _():
            z_first(slot, step)

        @pl.when(slot == 3)
        def _():
            x_first(XFIRST - 1, 3, 0, step)

        return carry

    lax.fori_loop(0, YS * 7, tick, 0)
    for slot in range(YS):
        source = lax.rem(y + YS - (0, 1, 3, 2)[slot], YS) * 2
        for way in range(2):
            first = 0 if slot else 1
            if way == 0 and slot < ZFIRST:
                for k in range(first, XS):
                    x_owe(slot, k).wait_recv()
                pieces = [x_arrived[slot, k] for k in range(XS)]
            else:
                u = slot if way else XFIRST - 1
                for k in range(first, ZS):
                    z_owe(u, slot, k).wait_recv()
                pieces = [z_arrived[u, k] for k in range(ZS)]
            total = pieces[0].astype(F32)
            for piece in pieces[1:]:
                total = total + piece.astype(F32)
            column = columns(source + way)
            key_out[:, column] = total[:, 0:HEAD]
            value_out[:, column] = total[:, HEAD : 2 * HEAD]

    for e in range(2):
        for k in range(1, ZS):
            z_copy(e, k).wait_send()
        for k in range(1, XS):
            x_copy(e, k).wait_send()
    for half in range(2):
        for slot in (1, 2):
            layer_copy(slot, half).wait_send()
        layer_relay(half).wait_send()
    swap.wait_send()

    def drain_z(v, carry):
        for side, hops in ((0, LONG), (1, SHORT)):
            for step in range(hops):
                z_hop(v, side, step).wait_send()
        for k in range(1, XS):
            x_owe(v, k).wait_send()

        @pl.when(v > 0)
        def _():
            x_owe(v, 0).wait_send()

        return carry

    lax.fori_loop(0, ZFIRST, drain_z, 0)

    def drain_x(u, carry):
        for kind in range(3):
            x_hop(u, kind).wait_send()
        slot = u - u // (XFIRST - 1)

        def one(k, carry):
            z_owe(u, slot, k).wait_send()
            return carry

        lax.fori_loop(1, ZS, one, 0)

        @pl.when(u > 0)
        def _():
            z_owe(u, slot, 0).wait_send()

        return carry

    lax.fori_loop(0, XFIRST, drain_x, 0)
    grad_copy.wait()


def shards(layer_input, query_columns, key_columns, value_columns, output_gradient):
    shape = jax.ShapeDtypeStruct
    vmem = pltpu.VMEM
    sems = pltpu.SemaphoreType.DMA
    wide = GROUP * HEAD
    far = pl.BlockSpec(memory_space=pl.ANY)
    near = pl.BlockSpec(memory_space=pltpu.VMEM)
    return pl.pallas_call(
        kernel,
        out_shape=(
            shape((ROWS, wide), BF16),
            shape((OUT, KEY_VALUE_HEADS * HEAD), F32),
            shape((OUT, KEY_VALUE_HEADS * HEAD), F32),
        ),
        in_specs=[far] * 5,
        out_specs=(far, near, near),
        scratch_shapes=[
            vmem((ROWS, wide), BF16),
            vmem((ROWS, wide), BF16),
            vmem((ROWS, HEAD), BF16),
            vmem((ROWS, HEAD), BF16),
            vmem((YS, ROWS, wide), BF16),
            vmem((ROWS, HEAD), BF16),
            vmem((ROWS, HEAD), F32),
            vmem((2, HEAD, HEAD), F32),
            vmem((2, 8, HEAD), F32),
            vmem((2, HEAD, HEAD), BF16),
            vmem((2, HEAD, HEAD), BF16),
            vmem((2, 8, HEAD), F32),
            vmem((HEAD + 8, HEAD), F32),
            vmem((ROWS, wide), BF16),
            vmem((GROUP, 2, BLOCK, BLOCK), BF16),
            vmem((ROWS, wide), F32),
            vmem((ROWS, wide), BF16),
            vmem((ROWS, wide), F32),
            vmem((ROWS, wide), BF16),
            vmem((2, HEAD, HEAD), F32),
            vmem((2, 8, HEAD), F32),
            vmem((ROWS, HEAD), F32),
            vmem((ROWS, HEAD), F32),
            vmem((2, 2, MESSAGE, HEAD), BF16),
            vmem((2, ZS, MESSAGE, HEAD), BF16),
            vmem((2, XS, MESSAGE, HEAD), BF16),
            vmem((YS, ZS, XS, OUT, ROWS), BF16),
            vmem((2, ROWS, 2 * HEAD), BF16),
            vmem((ZFIRST, 2, LONG, XS * OUT, 2 * HEAD), BF16),
            vmem((ZFIRST, 2, LONG + 1, XS * OUT, 2 * HEAD), BF16),
            vmem((XFIRST, 3, ZS * OUT, 2 * HEAD), BF16),
            vmem((XFIRST, 3, ZS * OUT, 2 * HEAD), BF16),
            vmem((ZFIRST, XS, OUT, 2 * HEAD), BF16),
            vmem((XFIRST, ZS, OUT, 2 * HEAD), BF16),
            vmem((ZFIRST, XS, OUT, 2 * HEAD), BF16),
            vmem((XFIRST, ZS, OUT, 2 * HEAD), BF16),
            sems((6,)),
            sems((2, ZS)),
            sems((2, ZS)),
            sems((2, XS)),
            sems((2, XS)),
            sems((YS, 2)),
            sems((YS, 2)),
            sems((1,)),
            sems((1,)),
            sems((ZFIRST, 2, LONG)),
            sems((ZFIRST, 2, LONG + 1)),
            sems((XFIRST, 3)),
            sems((XFIRST, 3)),
            sems((ZFIRST, XS)),
            sems((ZFIRST, XS)),
            sems((XFIRST, ZS)),
            sems((XFIRST, ZS)),
        ],
        compiler_params=pltpu.CompilerParams(
            collective_id=0, has_side_effects=True, vmem_limit_bytes=LIMIT
        ),
        name="backward",
    )(query_columns, output_gradient, key_columns, value_columns, layer_input)


def solution(mesh):
    placed = (P("ctx", "head"),) * 5
    return jax.shard_map(
        shards,
        mesh=mesh,
        in_specs=placed,
        out_specs=(P("ctx", "head"), P(("head", "ctx"), None), P(("head", "ctx"), None)),
        check_vma=False,
    )
```

```python
import jax
import jax.numpy as jnp
from jax import lax
from jax.experimental import pallas as pl
from jax.experimental.pallas import tpu as pltpu
from jax.sharding import PartitionSpec as P

QUERY_HEADS = 64
KEY_VALUE_HEADS = 8
GROUP = QUERY_HEADS // KEY_VALUE_HEADS
HEAD = 128
BLOCK = 256
ROWS = 512
XS = 4
ZS = 8
YS = 4
OUT = 32
MESSAGE = HEAD + 16
MESH = pl.DeviceIdType.MESH
F32 = jnp.float32
BF16 = jnp.bfloat16
HALF = 512
LONG = 4
SHORT = 3
NEAR = 5
ORDER = (
    ("x", 0, 0, 1),
    ("z", 0, 0, 1),
    ("turn", 1, 0, 0),
    ("x", 0, 1, 2),
    ("z", 0, 1, 2),
    ("turn", 2, 0, 0),
    ("x", 0, 2, 3),
    ("z", 0, 2, 3),
    ("z", 1, 0, 3),
    ("x", 1, 0, 3),
    ("turn", 3, 0, 0),
    ("z", 0, 3, 4),
    ("x", 0, 3, 4),
    ("z", 2, 0, 3),
    ("x", 2, 0, 3),
    ("z", 1, 3, 4),
    ("x", 1, 3, 4),
    ("z", 3, 0, 3),
    ("x", 3, 0, 3),
    ("z", 2, 3, 4),
    ("x", 2, 3, 4),
    ("z", 4, 0, 3),
    ("z", 3, 3, 4),
    ("x", 3, 3, 4),
    ("z", 4, 3, 4),
)
LIMIT = 60 << 20


def phi(raw):
    wide = raw.astype(F32)
    return jnp.where(wide > 0, wide + 1.0, jnp.exp(jnp.minimum(wide, 0.0))).astype(BF16)


def slope(raw):
    wide = raw.astype(F32)
    return jnp.where(wide > 0, 1.0, jnp.exp(jnp.minimum(wide, 0.0)))


def dot_nn(a, b):
    return lax.dot_general(a, b, (((1,), (0,)), ((), ())), preferred_element_type=F32)


def dot_nt(a, b):
    return lax.dot_general(a, b, (((1,), (1,)), ((), ())), preferred_element_type=F32)


def dot_tn(a, b):
    return lax.dot_general(a, b, (((0,), (0,)), ((), ())), preferred_element_type=F32)


def halves(value):
    high = value.astype(BF16)
    return high, (value - high.astype(F32)).astype(BF16)


def lower_mask():
    rows = lax.broadcasted_iota(jnp.int32, (BLOCK, BLOCK), 0)
    cols = lax.broadcasted_iota(jnp.int32, (BLOCK, BLOCK), 1)
    return cols <= rows


def remote(source, target, send, recv, device):
    return pltpu.make_async_remote_copy(
        src_ref=source,
        dst_ref=target,
        send_sem=send,
        recv_sem=recv,
        device_id=device,
        device_id_type=MESH,
    )


def pack(target, state, total):
    target[0:HEAD, :] = state.astype(BF16)
    high, low = halves(total)
    row = lax.broadcasted_iota(jnp.int32, (16, HEAD), 0)
    tail = jnp.where(row == 0, high.astype(F32), jnp.where(row == 1, low.astype(F32), 0.0))
    target[HEAD:MESSAGE, :] = tail.astype(BF16)


def parts(message):
    return message[0:HEAD, :], message[HEAD : HEAD + 1, :] + message[HEAD + 1 : HEAD + 2, :]


def kernel(
    query_hbm, cotangent_hbm, key_hbm, value_hbm, layer_hbm,
    query_grad_hbm, key_out, value_out,
    query, cotangent, key, value, layer,
    features, sums, states, totals, high, low, prior_total, rowsum,
    qf_all, scores_all, numer_all, g_all, c_all, grad_all,
    gstate, gtotal, dkey, dvalue,
    message, from_z, from_x,
    turned, paired, zsend, zrecv, xsend, xrecv, x_owed, z_owed, x_arrived, z_arrived, z_passed, z_joined,
    load, zs, zr, xs, xr, l_send, l_recv, f_send, f_recv,
    p_send, p_recv, q_send, q_recv, x_send, x_recv, z_send, z_recv, m_send, m_recv,
):
    me = lax.axis_index("ctx")
    head = lax.axis_index("head")
    x = me // ZS
    z = lax.rem(me, ZS)
    y = head // 2
    core = lax.rem(head, 2)
    sibling = {"head": head + 1 - 2 * core}
    z_line = [{"ctx": x * ZS + lax.rem(z + k, ZS)} for k in range(ZS)]
    x_line = [{"ctx": lax.rem(x + k, XS) * ZS + z} for k in range(XS)]
    y_line = [{"head": lax.rem(y + k, YS) * 2 + core} for k in range(YS)]

    loads = [
        pltpu.make_async_copy(source, target, load.at[i])
        for i, (source, target) in enumerate(
            (
                (key_hbm, key),
                (value_hbm, value),
                (query_hbm, query),
                (cotangent_hbm, cotangent),
                (layer_hbm, layer.at[0]),
            )
        )
    ]
    for copy in loads:
        copy.start()
    barrier = pltpu.get_barrier_semaphore()
    for device in z_line[1:] + x_line[1:] + y_line[1:] + [sibling]:
        pl.semaphore_signal(barrier, inc=1, device_id=device, device_id_type=MESH)

    def z_copy(e, k):
        return remote(message.at[e, 0], from_z.at[e, k], zs.at[e, k], zr.at[e, k], z_line[k])

    def x_copy(e, k):
        return remote(message.at[e, 1], from_x.at[e, k], xs.at[e, k], xr.at[e, k], x_line[k])

    def z_finish(e, state, total, reverse):
        line_state, line_total = state, total
        part_state, part_total = jnp.zeros_like(state), jnp.zeros_like(total)
        for k in range(1, ZS):
            z_copy(e, k).wait_recv()
            got_state, got_total = parts(from_z[e, k].astype(F32))
            line_state, line_total = line_state + got_state, line_total + got_total
            counts = (k > z) if reverse else (k <= z)
            part_state = part_state + jnp.where(counts, got_state, 0.0)
            part_total = part_total + jnp.where(counts, got_total, 0.0)
        pack(message.at[e, 1], line_state, line_total)
        for k in range(1, XS):
            x_copy(e, k).start()
        rowsum[0:HEAD, :] = part_state
        rowsum[HEAD : HEAD + 8, :] = jnp.broadcast_to(part_total, (8, HEAD))

    def x_finish(e, reverse):
        state, total = rowsum[0:HEAD, :], rowsum[HEAD : HEAD + 1, :]
        for k in range(1, XS):
            x_copy(e, k).wait_recv()
            got_state, got_total = parts(from_x[e, k].astype(F32))
            counts = (k > x) if reverse else (k <= x)
            state = state + jnp.where(counts, got_state, 0.0)
            total = total + jnp.where(counts, got_total, 0.0)
        return state, total

    mask = lower_mask()
    blocks = [pl.ds(b * BLOCK, BLOCK) for b in range(2)]

    loads[0].wait()
    loads[1].wait()
    for b in range(2):
        kf = phi(key[blocks[b], :])
        features[blocks[b], :] = kf
        states[b] = dot_tn(kf, value[blocks[b], :])
        totals[b] = jnp.broadcast_to(
            jnp.sum(kf.astype(F32), axis=0, keepdims=True), (8, HEAD)
        )
    own_total = totals[0, 0:1, :] + totals[1, 0:1, :]
    pack(message.at[0, 0], states[0] + states[1], own_total)
    pl.semaphore_wait(barrier, ZS - 1 + XS - 1 + YS - 1 + 1)
    for k in range(1, ZS):
        z_copy(0, k).start()

    def layer_copy(slot, half):
        part = pl.ds(half * HALF, HALF)
        return remote(
            layer.at[0, :, part],
            layer.at[slot, :, part],
            l_send.at[slot, half],
            l_recv.at[slot, half],
            y_line[YS - 1 if slot == 1 else 1],
        )

    def layer_relay(half):
        part = pl.ds(half * HALF, HALF)
        return remote(
            layer.at[1 + core, :, part],
            layer.at[3, :, part],
            l_send.at[3, half],
            l_recv.at[3, half],
            {"head": lax.rem(y + YS - 1 + 2 * core, YS) * 2 + core},
        )

    def turn(slot, half):
        def one(i, carry):
            j = half * 4 + i
            block = layer[slot, :, pl.ds(pl.multiple_of(j * HEAD, HEAD), HEAD)].T
            for q in range(4):
                turned[slot, lax.rem(j, 2) * 4 + q, j // 2] = block[q * OUT : (q + 1) * OUT, :]
            return carry

        lax.fori_loop(0, 4, one, 0)

    loads[4].wait()
    for slot in (1, 2):
        layer_copy(slot, 0).start()

    triangle = jnp.where(mask, 1.0, 0.0).astype(BF16)
    for b in range(2):
        sums[blocks[b], :] = dot_nn(triangle, features[blocks[b], :])
    gstate[...] = jnp.zeros_like(gstate)
    gtotal[...] = jnp.zeros_like(gtotal)
    dkey[...] = jnp.zeros_like(dkey)
    dvalue[...] = jnp.zeros_like(dvalue)

    def columns(h):
        return pl.ds(pl.multiple_of(h * HEAD, HEAD), HEAD)

    def inside(h, carry):
        at = columns(h)
        for b in range(2):
            qf = phi(query[blocks[b], at])
            qf_all[blocks[b], at] = qf
            scores = jnp.where(mask, dot_nt(qf, features[blocks[b], :]), 0.0).astype(BF16)
            scores_all[h, b] = scores
            numer_all[blocks[b], at] = dot_nn(scores, value[blocks[b], :])
        return carry

    def forward_pass(h, carry):
        at = columns(h)
        for b in range(2):
            qf = qf_all[blocks[b], at]
            wide = qf.astype(F32)
            den = jnp.sum(wide * sums[blocks[b], :], axis=1, keepdims=True)
            numer = numer_all[blocks[b], at] + dot_nn(qf, high[b]) + dot_nn(qf, low[b])
            inverse = 1.0 / den
            wide_cot = cotangent[blocks[b], at].astype(F32)
            g = (wide_cot * inverse).astype(BF16)
            c = -jnp.sum(wide_cot * numer, axis=1, keepdims=True) * inverse * inverse
            c = jnp.broadcast_to(c, (BLOCK, HEAD))
            g_all[blocks[b], at] = g
            c_all[blocks[b], at] = c
            gstate[b] += dot_tn(qf, g)
            gtotal[b] += jnp.broadcast_to(jnp.sum(wide * c, axis=0, keepdims=True), (8, HEAD))
        return carry

    def backward_pass(h, carry):
        at = columns(h)
        for b in range(2):
            g = g_all[blocks[b], at]
            qf = qf_all[blocks[b], at]
            c = c_all[blocks[b], at]
            kf = features[blocks[b], :]
            dscores = dot_nt(g, value[blocks[b], :]) + jnp.concatenate([c, c], axis=1)
            dscores = jnp.where(mask, dscores, 0.0).astype(BF16)
            dqf = (
                dot_nt(g, high[b])
                + dot_nt(g, low[b])
                + c * prior_total[b, 0:1, :]
                + dot_nn(dscores, kf)
            )
            grad_all[blocks[b], at] = (dqf * slope(query[blocks[b], at])).astype(BF16)
            dkey[blocks[b], :] += dot_tn(dscores, qf)
            dvalue[blocks[b], :] += dot_tn(scores_all[h, b], g)
        return carry

    loads[2].wait()
    lax.fori_loop(0, GROUP // 2, inside, 0)
    z_finish(0, states[0] + states[1], own_total, False)
    for slot in (1, 2):
        layer_copy(slot, 1).start()
    lax.fori_loop(GROUP // 2, GROUP, inside, 0)
    turn(0, 0)
    turn(0, 1)
    loads[3].wait()
    state, total = x_finish(0, False)
    for b in range(2):
        high[b], low[b] = halves(state)
        prior_total[b] = jnp.broadcast_to(total, (8, HEAD))
        sums[blocks[b], :] += total
        state = state + states[b]
        total = total + totals[b, 0:1, :]
    lax.fori_loop(0, GROUP, forward_pass, 0)
    own_gtotal = gtotal[0, 0:1, :] + gtotal[1, 0:1, :]
    pack(message.at[1, 0], gstate[0] + gstate[1], own_gtotal)
    for k in range(1, ZS):
        z_copy(1, k).start()
    for slot in (1, 2):
        layer_copy(slot, 0).wait_recv()
    layer_relay(0).start()
    lax.fori_loop(0, GROUP // 2, backward_pass, 0)
    turn(1, 0)
    turn(2, 0)
    z_finish(1, gstate[0] + gstate[1], own_gtotal, True)
    lax.fori_loop(GROUP // 2, GROUP, backward_pass, 0)
    grad_copy = pltpu.make_async_copy(grad_all, query_grad_hbm, load.at[5])
    grad_copy.start()
    for slot in (1, 2):
        layer_copy(slot, 1).wait_recv()
    layer_relay(1).start()
    later, later_total = x_finish(1, True)
    for b in (1, 0):
        later_high, later_low = halves(later)
        v = value[blocks[b], :]
        kf = features[blocks[b], :]
        dk = dkey[blocks[b], :] + dot_nt(v, later_high) + dot_nt(v, later_low) + later_total
        paired[core, blocks[b], 0:HEAD] = (dk * slope(key[blocks[b], :])).astype(BF16)
        dv = dvalue[blocks[b], :] + dot_nn(kf, later_high) + dot_nn(kf, later_low)
        paired[core, blocks[b], HEAD : 2 * HEAD] = dv.astype(BF16)
        later = later + gstate[b]
        later_total = later_total + gtotal[b, 0:1, :]

    swap = remote(paired.at[core], paired.at[core], f_send.at[0], f_recv.at[0], sibling)
    swap_in = remote(paired.at[1 - core], paired.at[1 - core], f_send.at[0], f_recv.at[0], sibling)
    swap.start()
    swap_in.wait_recv()

    def away_of(slot):
        return slot + (slot // 2) * (1 - 2 * lax.rem(slot, 2))

    def z_local(slot, way, to):
        return dot_nn(turned[slot, to].reshape(XS * OUT, ROWS), paired[way])

    def x_local(slot, way, to):
        return dot_nn(turned[slot, :, to].reshape(ZS * OUT, ROWS), paired[way])

    def z_hop(v, side, step):
        sign = (1 - 2 * lax.rem(v, 2)) * (1 - 2 * side)
        return remote(
            zsend.at[v, side, step],
            zrecv.at[v, side, step + 1],
            p_send.at[v, side, step],
            p_recv.at[v, side, step + 1],
            {"ctx": x * ZS + lax.rem(z + ZS + sign, ZS)},
        )

    def x_hop(u, kind):
        sign = 1 - 2 * lax.rem(u, 2)
        if kind == 2:
            sign = -sign
        return remote(
            xsend.at[u, kind],
            xrecv.at[u, kind],
            q_send.at[u, kind],
            q_recv.at[u, kind],
            {"ctx": lax.rem(x + XS + sign, XS) * ZS + z},
        )

    def x_owe(v, k):
        to = lax.rem(x + k, XS)
        return remote(
            x_owed.at[v, to],
            x_arrived.at[v, k],
            x_send.at[v, k],
            x_recv.at[v, k],
            {"ctx": to * ZS + z, "head": lax.rem(y + away_of(v), YS) * 2 + core},
        )

    def z_at(k):
        return lax.rem(z + ZS + k, ZS)

    def z_owe(u, kind):
        if kind < 3:
            to = z_at((0, 1, -1)[kind])
            source = z_owed.at[u, to]
        else:
            to = z_at((2, -2)[kind - 3])
            source = z_joined.at[u, kind - 3]
        return remote(
            source,
            z_arrived.at[u, kind],
            z_send.at[u, kind],
            z_recv.at[u, kind],
            {"ctx": x * ZS + to, "head": lax.rem(y + away_of(u), YS) * 2 + core},
        )

    def z_pass(u, kind):
        sign = 1 - 2 * lax.rem(u, 2)
        chunk = z_at((3, -3, 4)[kind])
        to = z_at((1, -1, 2 * sign)[kind])
        return remote(
            z_owed.at[u, chunk],
            z_passed.at[u, kind],
            m_send.at[u, kind],
            m_recv.at[u, kind],
            {"ctx": x * ZS + to},
        )

    def z_step(step):
        def run(v, carry):
            if step == LONG:
                total = z_local(v, 0, z)
                z_hop(v, 0, LONG - 1).wait_recv()
                z_hop(v, 1, SHORT - 1).wait_recv()
                total = total + zrecv[v, 0, LONG].astype(F32) + zrecv[v, 1, SHORT].astype(F32)
                x_owed[v] = total.astype(BF16).reshape(XS, OUT, 2 * HEAD)
                for k in range(1, XS):
                    x_owe(v, k).start()

                @pl.when(v == 0)
                def _():
                    x_arrived[0, 0] = x_owed[0, x]

                @pl.when(v > 0)
                def _():
                    x_owe(v, 0).start()

                return carry
            for side, hops in ((0, LONG), (1, SHORT)):
                if step >= hops:
                    continue
                sign = (1 - 2 * lax.rem(v, 2)) * (1 - 2 * side)
                to = lax.rem(z + ZS + sign * (hops - step), ZS)
                both = z_local(v, 0, to)
                if step > 0:
                    z_hop(v, side, step - 1).wait_recv()
                    both = both + zrecv[v, side, step].astype(F32)
                zsend[v, side, step] = both.astype(BF16)
                z_hop(v, side, step).start()
            return carry

        return run

    def x_step(step):
        def run(u, carry):
            slot, way = u, 1
            sign = 1 - 2 * lax.rem(u, 2)
            if step == 0:
                xsend[u, 0] = x_local(slot, way, lax.rem(x + 2, XS)).astype(BF16)
                x_hop(u, 0).start()
                xsend[u, 2] = x_local(slot, way, lax.rem(x + XS - sign, XS)).astype(BF16)
                x_hop(u, 2).start()
                return carry
            if step == 1:
                mine = x_local(slot, way, lax.rem(x + XS + sign, XS))
                x_hop(u, 0).wait_recv()
                xsend[u, 1] = (mine + xrecv[u, 0].astype(F32)).astype(BF16)
                x_hop(u, 1).start()
                return carry
            if step == 3:
                for kind in range(3):
                    z_pass(u, kind).wait_recv()
                extra = z_passed[u, 2].astype(F32)
                for side in range(2):
                    total = z_owed[u, z_at((2, -2)[side])].astype(F32)
                    total = total + z_passed[u, side].astype(F32)
                    total = total + jnp.where(lax.rem(u, 2) == side, extra, 0.0)
                    z_joined[u, side] = total.astype(BF16)
                    z_owe(u, 3 + side).start()
                return carry
            total = x_local(slot, way, x)
            x_hop(u, 1).wait_recv()
            x_hop(u, 2).wait_recv()
            total = total + xrecv[u, 1].astype(F32) + xrecv[u, 2].astype(F32)
            z_owed[u] = total.astype(BF16).reshape(ZS, OUT, 2 * HEAD)
            for kind in (2, 0, 1):
                z_pass(u, kind).start()
            for kind in (1, 2):
                z_owe(u, kind).start()

            @pl.when(u == 0)
            def _():
                z_arrived[0, 0] = z_owed[0, z]

            @pl.when(u > 0)
            def _():
                z_owe(u, 0).start()

            return carry

        return run

    for kind, step, first, end in ORDER:
        if kind == "x":
            lax.fori_loop(first, end, x_step(step), 0)
        elif kind == "z":
            lax.fori_loop(first, end, z_step(step), 0)
        else:
            if step == 3:
                layer_relay(0).wait_recv()
                turn(3, 0)
                layer_relay(1).wait_recv()
            turn(step, 1)
    for e in range(2):
        for k in range(1, ZS):
            z_copy(e, k).wait_send()
        for k in range(1, XS):
            x_copy(e, k).wait_send()
    for half in range(2):
        for slot in (1, 2):
            layer_copy(slot, half).wait_send()
        layer_relay(half).wait_send()
    swap.wait_send()

    def drain(u, carry):
        for side, hops in ((0, LONG), (1, SHORT)):
            for step in range(hops):
                z_hop(u, side, step).wait_send()
        for kind in range(3):
            x_hop(u, kind).wait_send()
            z_pass(u, kind).wait_send()
        return carry

    lax.fori_loop(0, YS, drain, 0)
    grad_copy.wait()
    for slot in range(YS):
        source = lax.rem(y + YS - (0, 1, 3, 2)[slot], YS) * 2
        for way in range(2):
            first = 0 if slot else 1
            if way == 0:
                for k in range(first, XS):
                    x_owe(slot, k).wait_recv()
                pieces = [x_arrived[slot, k] for k in range(XS)]
            else:
                for kind in range(first, NEAR):
                    z_owe(slot, kind).wait_recv()
                pieces = [z_arrived[slot, kind] for kind in range(NEAR)]
            total = pieces[0].astype(F32)
            for piece in pieces[1:]:
                total = total + piece.astype(F32)
            column = columns(source + way)
            key_out[:, column] = total[:, 0:HEAD]
            value_out[:, column] = total[:, HEAD : 2 * HEAD]

    def drain_last(u, carry):
        for k in range(1, XS):
            x_owe(u, k).wait_send()
        for kind in range(1, NEAR):
            z_owe(u, kind).wait_send()

        @pl.when(u > 0)
        def _():
            x_owe(u, 0).wait_send()
            z_owe(u, 0).wait_send()

        return carry

    lax.fori_loop(0, YS, drain_last, 0)


def shards(layer_input, query_columns, key_columns, value_columns, output_gradient):
    shape = jax.ShapeDtypeStruct
    vmem = pltpu.VMEM
    sems = pltpu.SemaphoreType.DMA
    wide = GROUP * HEAD
    far = pl.BlockSpec(memory_space=pl.ANY)
    near = pl.BlockSpec(memory_space=pltpu.VMEM)
    return pl.pallas_call(
        kernel,
        out_shape=(
            shape((ROWS, wide), BF16),
            shape((OUT, KEY_VALUE_HEADS * HEAD), F32),
            shape((OUT, KEY_VALUE_HEADS * HEAD), F32),
        ),
        in_specs=[far] * 5,
        out_specs=(far, near, near),
        scratch_shapes=[
            vmem((ROWS, wide), BF16),
            vmem((ROWS, wide), BF16),
            vmem((ROWS, HEAD), BF16),
            vmem((ROWS, HEAD), BF16),
            vmem((YS, ROWS, wide), BF16),
            vmem((ROWS, HEAD), BF16),
            vmem((ROWS, HEAD), F32),
            vmem((2, HEAD, HEAD), F32),
            vmem((2, 8, HEAD), F32),
            vmem((2, HEAD, HEAD), BF16),
            vmem((2, HEAD, HEAD), BF16),
            vmem((2, 8, HEAD), F32),
            vmem((HEAD + 8, HEAD), F32),
            vmem((ROWS, wide), BF16),
            vmem((GROUP, 2, BLOCK, BLOCK), BF16),
            vmem((ROWS, wide), F32),
            vmem((ROWS, wide), BF16),
            vmem((ROWS, wide), F32),
            vmem((ROWS, wide), BF16),
            vmem((2, HEAD, HEAD), F32),
            vmem((2, 8, HEAD), F32),
            vmem((ROWS, HEAD), F32),
            vmem((ROWS, HEAD), F32),
            vmem((2, 2, MESSAGE, HEAD), BF16),
            vmem((2, ZS, MESSAGE, HEAD), BF16),
            vmem((2, XS, MESSAGE, HEAD), BF16),
            vmem((YS, ZS, XS, OUT, ROWS), BF16),
            vmem((2, ROWS, 2 * HEAD), BF16),
            vmem((YS, 2, LONG, XS * OUT, 2 * HEAD), BF16),
            vmem((YS, 2, LONG + 1, XS * OUT, 2 * HEAD), BF16),
            vmem((YS, 3, ZS * OUT, 2 * HEAD), BF16),
            vmem((YS, 3, ZS * OUT, 2 * HEAD), BF16),
            vmem((YS, XS, OUT, 2 * HEAD), BF16),
            vmem((YS, ZS, OUT, 2 * HEAD), BF16),
            vmem((YS, XS, OUT, 2 * HEAD), BF16),
            vmem((YS, NEAR, OUT, 2 * HEAD), BF16),
            vmem((YS, 3, OUT, 2 * HEAD), BF16),
            vmem((YS, 2, OUT, 2 * HEAD), BF16),
            sems((6,)),
            sems((2, ZS)),
            sems((2, ZS)),
            sems((2, XS)),
            sems((2, XS)),
            sems((YS, 2)),
            sems((YS, 2)),
            sems((1,)),
            sems((1,)),
            sems((YS, 2, LONG)),
            sems((YS, 2, LONG + 1)),
            sems((YS, 3)),
            sems((YS, 3)),
            sems((YS, XS)),
            sems((YS, XS)),
            sems((YS, NEAR)),
            sems((YS, NEAR)),
            sems((YS, 3)),
            sems((YS, 3)),
        ],
        compiler_params=pltpu.CompilerParams(
            collective_id=0, has_side_effects=True, vmem_limit_bytes=LIMIT
        ),
        name="backward",
    )(query_columns, output_gradient, key_columns, value_columns, layer_input)


def solution(mesh):
    placed = (P("ctx", "head"),) * 5
    return jax.shard_map(
        shards,
        mesh=mesh,
        in_specs=placed,
        out_specs=(P("ctx", "head"), P(("head", "ctx"), None), P(("head", "ctx"), None)),
        check_vma=False,
    )
```

```python
import jax
import jax.numpy as jnp
from jax import lax
from jax.experimental import pallas as pl
from jax.experimental.pallas import tpu as pltpu
from jax.sharding import PartitionSpec as P

QUERY_HEADS = 64
KEY_VALUE_HEADS = 8
GROUP = QUERY_HEADS // KEY_VALUE_HEADS
HEAD = 128
BLOCK = 256
ROWS = 512
XS = 4
ZS = 8
YS = 4
OUT = 32
MESSAGE = HEAD + 16
MESH = pl.DeviceIdType.MESH
F32 = jnp.float32
BF16 = jnp.bfloat16
HALF = 512
LONG = 4
SHORT = 3
NEAR = 5
ORDER = (
    ("x", 0, 0, 1),
    ("z", 0, 0, 1),
    ("x", 0, 1, 2),
    ("z", 0, 1, 2),
    ("x", 0, 2, 3),
    ("z", 0, 2, 3),
    ("turn", 0, 0, 0),
    ("z", 1, 0, 3),
    ("x", 1, 0, 2),
    ("turn", 1, 0, 0),
    ("z", 0, 3, 4),
    ("x", 0, 3, 4),
    ("x", 1, 2, 3),
    ("z", 2, 0, 3),
    ("z", 1, 3, 4),
    ("x", 2, 0, 3),
    ("x", 1, 3, 4),
    ("z", 3, 0, 3),
    ("z", 2, 3, 4),
    ("x", 3, 0, 3),
    ("x", 2, 3, 4),
    ("z", 4, 0, 3),
    ("z", 3, 3, 4),
    ("x", 3, 3, 4),
    ("z", 4, 3, 4),
)
EARLY = 6
LIMIT = 52 << 20


def phi(raw):
    wide = raw.astype(F32)
    return jnp.where(wide > 0, wide + 1.0, jnp.exp(jnp.minimum(wide, 0.0))).astype(BF16)


def slope(raw):
    wide = raw.astype(F32)
    return jnp.where(wide > 0, 1.0, jnp.exp(jnp.minimum(wide, 0.0)))


def dot_nn(a, b):
    return lax.dot_general(a, b, (((1,), (0,)), ((), ())), preferred_element_type=F32)


def dot_nt(a, b):
    return lax.dot_general(a, b, (((1,), (1,)), ((), ())), preferred_element_type=F32)


def dot_tn(a, b):
    return lax.dot_general(a, b, (((0,), (0,)), ((), ())), preferred_element_type=F32)


def halves(value):
    high = value.astype(BF16)
    return high, (value - high.astype(F32)).astype(BF16)


def lower_mask():
    rows = lax.broadcasted_iota(jnp.int32, (BLOCK, BLOCK), 0)
    cols = lax.broadcasted_iota(jnp.int32, (BLOCK, BLOCK), 1)
    return cols <= rows


def remote(source, target, send, recv, device):
    return pltpu.make_async_remote_copy(
        src_ref=source,
        dst_ref=target,
        send_sem=send,
        recv_sem=recv,
        device_id=device,
        device_id_type=MESH,
    )


def pack(target, state, total):
    target[0:HEAD, :] = state.astype(BF16)
    high, low = halves(total)
    row = lax.broadcasted_iota(jnp.int32, (16, HEAD), 0)
    tail = jnp.where(row == 0, high.astype(F32), jnp.where(row == 1, low.astype(F32), 0.0))
    target[HEAD:MESSAGE, :] = tail.astype(BF16)


def parts(message):
    return message[0:HEAD, :], message[HEAD : HEAD + 1, :] + message[HEAD + 1 : HEAD + 2, :]


def kernel(
    query_hbm, cotangent_hbm, key_hbm, value_hbm, layer_hbm,
    query_grad_hbm, key_out, value_out,
    query, cotangent, key, value, layer,
    features, sums, states, totals, high, low, prior_total, rowsum,
    qf_all, scores_all, numer_all, g_all, c_all, grad_all,
    gstate, gtotal, dkey, dvalue,
    message, from_z, from_x,
    turned, paired, zsend, zrecv, xsend, xrecv, x_owed, z_owed, x_arrived, z_arrived, z_passed, z_joined,
    load, zs, zr, xs, xr, l_send, l_recv, f_send, f_recv,
    p_send, p_recv, q_send, q_recv, x_send, x_recv, z_send, z_recv, m_send, m_recv,
):
    me = lax.axis_index("ctx")
    head = lax.axis_index("head")
    x = me // ZS
    z = lax.rem(me, ZS)
    y = head // 2
    core = lax.rem(head, 2)
    sibling = {"head": head + 1 - 2 * core}
    z_line = [{"ctx": x * ZS + lax.rem(z + k, ZS)} for k in range(ZS)]
    x_line = [{"ctx": lax.rem(x + k, XS) * ZS + z} for k in range(XS)]
    y_line = [{"head": lax.rem(y + k, YS) * 2 + core} for k in range(YS)]

    loads = [
        pltpu.make_async_copy(source, target, load.at[i])
        for i, (source, target) in enumerate(
            (
                (key_hbm, key),
                (value_hbm, value),
                (query_hbm, query),
                (cotangent_hbm, cotangent),
                (layer_hbm, layer.at[0]),
            )
        )
    ]
    loads[0].start()
    loads[1].start()
    barrier = pltpu.get_barrier_semaphore()
    for device in z_line[1:] + x_line[1:] + y_line[1:] + [sibling]:
        pl.semaphore_signal(barrier, inc=1, device_id=device, device_id_type=MESH)
    for copy in loads[2:]:
        copy.start()

    def z_copy(e, k):
        return remote(message.at[e, 0], from_z.at[e, k], zs.at[e, k], zr.at[e, k], z_line[k])

    def x_copy(e, k):
        return remote(message.at[e, 1], from_x.at[e, k], xs.at[e, k], xr.at[e, k], x_line[k])

    def z_finish(e, state, total, reverse):
        line_state, line_total = state, total
        part_state, part_total = jnp.zeros_like(state), jnp.zeros_like(total)
        for k in range(1, ZS):
            z_copy(e, k).wait_recv()
            got_state, got_total = parts(from_z[e, k].astype(F32))
            line_state, line_total = line_state + got_state, line_total + got_total
            counts = (k > z) if reverse else (k <= z)
            part_state = part_state + jnp.where(counts, got_state, 0.0)
            part_total = part_total + jnp.where(counts, got_total, 0.0)
        pack(message.at[e, 1], line_state, line_total)
        for k in range(1, XS):
            x_copy(e, k).start()
        rowsum[0:HEAD, :] = part_state
        rowsum[HEAD : HEAD + 8, :] = jnp.broadcast_to(part_total, (8, HEAD))

    def x_finish(e, reverse):
        state, total = rowsum[0:HEAD, :], rowsum[HEAD : HEAD + 1, :]
        for k in range(1, XS):
            x_copy(e, k).wait_recv()
            got_state, got_total = parts(from_x[e, k].astype(F32))
            counts = (k > x) if reverse else (k <= x)
            state = state + jnp.where(counts, got_state, 0.0)
            total = total + jnp.where(counts, got_total, 0.0)
        return state, total

    mask = lower_mask()
    blocks = [pl.ds(b * BLOCK, BLOCK) for b in range(2)]

    loads[0].wait()
    loads[1].wait()
    for b in range(2):
        kf = phi(key[blocks[b], :])
        features[blocks[b], :] = kf
        states[b] = dot_tn(kf, value[blocks[b], :])
        totals[b] = jnp.broadcast_to(
            jnp.sum(kf.astype(F32), axis=0, keepdims=True), (8, HEAD)
        )
    own_total = totals[0, 0:1, :] + totals[1, 0:1, :]
    pack(message.at[0, 0], states[0] + states[1], own_total)
    pl.semaphore_wait(barrier, ZS - 1 + XS - 1 + YS - 1 + 1)
    for k in range(1, ZS):
        z_copy(0, k).start()

    def layer_copy(slot, half):
        part = pl.ds(half * HALF, HALF)
        return remote(
            layer.at[0, :, part],
            layer.at[slot, :, part],
            l_send.at[slot, half],
            l_recv.at[slot, half],
            y_line[YS - 1 if slot == 1 else 1],
        )

    def layer_relay(half):
        part = pl.ds(half * HALF, HALF)
        return remote(
            layer.at[1 + core, :, part],
            layer.at[3, :, part],
            l_send.at[3, half],
            l_recv.at[3, half],
            {"head": lax.rem(y + YS - 1 + 2 * core, YS) * 2 + core},
        )

    def turn(slot, half):
        def one(i, carry):
            j = half * 4 + i
            block = layer[slot, :, pl.ds(pl.multiple_of(j * HEAD, HEAD), HEAD)].T
            for q in range(4):
                turned[slot, lax.rem(j, 2) * 4 + q, j // 2] = block[q * OUT : (q + 1) * OUT, :]
            return carry

        lax.fori_loop(0, 4, one, 0)

    loads[4].wait()
    for slot in (1, 2):
        layer_copy(slot, 0).start()

    triangle = jnp.where(mask, 1.0, 0.0).astype(BF16)
    for b in range(2):
        sums[blocks[b], :] = dot_nn(triangle, features[blocks[b], :])
    gstate[...] = jnp.zeros_like(gstate)
    gtotal[...] = jnp.zeros_like(gtotal)
    dkey[...] = jnp.zeros_like(dkey)
    dvalue[...] = jnp.zeros_like(dvalue)

    def columns(h):
        return pl.ds(pl.multiple_of(h * HEAD, HEAD), HEAD)

    def inside(h, carry):
        at = columns(h)
        for b in range(2):
            qf = phi(query[blocks[b], at])
            qf_all[blocks[b], at] = qf
            scores = jnp.where(mask, dot_nt(qf, features[blocks[b], :]), 0.0).astype(BF16)
            scores_all[h, b] = scores
            numer_all[blocks[b], at] = dot_nn(scores, value[blocks[b], :])
        return carry

    def forward_pass(h, carry):
        at = columns(h)
        for b in range(2):
            qf = qf_all[blocks[b], at]
            wide = qf.astype(F32)
            den = jnp.sum(wide * sums[blocks[b], :], axis=1, keepdims=True)
            numer = numer_all[blocks[b], at] + dot_nn(qf, high[b]) + dot_nn(qf, low[b])
            inverse = 1.0 / den
            wide_cot = cotangent[blocks[b], at].astype(F32)
            g = (wide_cot * inverse).astype(BF16)
            c = -jnp.sum(wide_cot * numer, axis=1, keepdims=True) * inverse * inverse
            c = jnp.broadcast_to(c, (BLOCK, HEAD))
            g_all[blocks[b], at] = g
            c_all[blocks[b], at] = c
            gstate[b] += dot_tn(qf, g)
            gtotal[b] += jnp.broadcast_to(jnp.sum(wide * c, axis=0, keepdims=True), (8, HEAD))
        return carry

    def backward_pass(h, carry):
        at = columns(h)
        for b in range(2):
            g = g_all[blocks[b], at]
            qf = qf_all[blocks[b], at]
            c = c_all[blocks[b], at]
            kf = features[blocks[b], :]
            dscores = dot_nt(g, value[blocks[b], :]) + jnp.concatenate([c, c], axis=1)
            dscores = jnp.where(mask, dscores, 0.0).astype(BF16)
            dqf = (
                dot_nt(g, high[b])
                + dot_nt(g, low[b])
                + c * prior_total[b, 0:1, :]
                + dot_nn(dscores, kf)
            )
            grad_all[blocks[b], at] = (dqf * slope(query[blocks[b], at])).astype(BF16)
            dkey[blocks[b], :] += dot_tn(dscores, qf)
            dvalue[blocks[b], :] += dot_tn(scores_all[h, b], g)
        return carry

    loads[2].wait()
    lax.fori_loop(0, GROUP // 2, inside, 0)
    z_finish(0, states[0] + states[1], own_total, False)
    for slot in (1, 2):
        layer_copy(slot, 1).start()
    lax.fori_loop(GROUP // 2, GROUP, inside, 0)
    turn(0, 0)
    turn(0, 1)
    loads[3].wait()
    state, total = x_finish(0, False)
    for b in range(2):
        high[b], low[b] = halves(state)
        prior_total[b] = jnp.broadcast_to(total, (8, HEAD))
        sums[blocks[b], :] += total
        state = state + states[b]
        total = total + totals[b, 0:1, :]
    lax.fori_loop(0, GROUP, forward_pass, 0)
    own_gtotal = gtotal[0, 0:1, :] + gtotal[1, 0:1, :]
    pack(message.at[1, 0], gstate[0] + gstate[1], own_gtotal)
    for k in range(1, ZS):
        z_copy(1, k).start()
    for slot in (1, 2):
        layer_copy(slot, 0).wait_recv()
    layer_relay(0).start()
    lax.fori_loop(0, EARLY, backward_pass, 0)
    turn(1, 0)
    turn(2, 0)
    z_finish(1, gstate[0] + gstate[1], own_gtotal, True)
    lax.fori_loop(EARLY, GROUP, backward_pass, 0)
    grad_copy = pltpu.make_async_copy(grad_all, query_grad_hbm, load.at[5])
    grad_copy.start()
    for slot in (1, 2):
        layer_copy(slot, 1).wait_recv()
    layer_relay(1).start()
    turn(1, 1)
    turn(2, 1)
    later, later_total = x_finish(1, True)
    for b in (1, 0):
        later_high, later_low = halves(later)
        v = value[blocks[b], :]
        kf = features[blocks[b], :]
        dk = dkey[blocks[b], :] + dot_nt(v, later_high) + dot_nt(v, later_low) + later_total
        paired[core, blocks[b], 0:HEAD] = (dk * slope(key[blocks[b], :])).astype(BF16)
        dv = dvalue[blocks[b], :] + dot_nn(kf, later_high) + dot_nn(kf, later_low)
        paired[core, blocks[b], HEAD : 2 * HEAD] = dv.astype(BF16)
        later = later + gstate[b]
        later_total = later_total + gtotal[b, 0:1, :]

    swap = remote(paired.at[core], paired.at[core], f_send.at[0], f_recv.at[0], sibling)
    swap_in = remote(paired.at[1 - core], paired.at[1 - core], f_send.at[0], f_recv.at[0], sibling)
    swap.start()
    swap_in.wait_recv()

    def away_of(slot):
        return slot + (slot // 2) * (1 - 2 * lax.rem(slot, 2))

    def z_local(slot, way, to):
        return dot_nn(turned[slot, to].reshape(XS * OUT, ROWS), paired[way])

    def x_local(slot, way, to):
        return dot_nn(turned[slot, :, to].reshape(ZS * OUT, ROWS), paired[way])

    def z_hop(v, side, step):
        sign = (1 - 2 * lax.rem(v, 2)) * (1 - 2 * side)
        return remote(
            zsend.at[v, side, step],
            zrecv.at[v, side, step + 1],
            p_send.at[v, side, step],
            p_recv.at[v, side, step + 1],
            {"ctx": x * ZS + lax.rem(z + ZS + sign, ZS)},
        )

    def x_hop(u, kind):
        sign = 1 - 2 * lax.rem(u, 2)
        if kind == 2:
            sign = -sign
        return remote(
            xsend.at[u, kind],
            xrecv.at[u, kind],
            q_send.at[u, kind],
            q_recv.at[u, kind],
            {"ctx": lax.rem(x + XS + sign, XS) * ZS + z},
        )

    def x_owe(v, k):
        to = lax.rem(x + k, XS)
        return remote(
            x_owed.at[v, to],
            x_arrived.at[v, k],
            x_send.at[v, k],
            x_recv.at[v, k],
            {"ctx": to * ZS + z, "head": lax.rem(y + away_of(v), YS) * 2 + core},
        )

    def z_at(k):
        return lax.rem(z + ZS + k, ZS)

    def z_owe(u, kind):
        if kind < 3:
            to = z_at((0, 1, -1)[kind])
            source = z_owed.at[u, to]
        else:
            to = z_at((2, -2)[kind - 3])
            source = z_joined.at[u, kind - 3]
        return remote(
            source,
            z_arrived.at[u, kind],
            z_send.at[u, kind],
            z_recv.at[u, kind],
            {"ctx": x * ZS + to, "head": lax.rem(y + away_of(u), YS) * 2 + core},
        )

    def z_pass(u, kind):
        sign = 1 - 2 * lax.rem(u, 2)
        chunk = z_at((3, -3, 4)[kind])
        to = z_at((1, -1, 2 * sign)[kind])
        return remote(
            z_owed.at[u, chunk],
            z_passed.at[u, kind],
            m_send.at[u, kind],
            m_recv.at[u, kind],
            {"ctx": x * ZS + to},
        )

    def z_step(step):
        def run(v, carry):
            if step == LONG:
                total = z_local(v, 0, z)
                z_hop(v, 0, LONG - 1).wait_recv()
                z_hop(v, 1, SHORT - 1).wait_recv()
                total = total + zrecv[v, 0, LONG].astype(F32) + zrecv[v, 1, SHORT].astype(F32)
                x_owed[v] = total.astype(BF16).reshape(XS, OUT, 2 * HEAD)
                for k in range(1, XS):
                    x_owe(v, k).start()

                @pl.when(v == 0)
                def _():
                    x_arrived[0, 0] = x_owed[0, x]

                @pl.when(v > 0)
                def _():
                    x_owe(v, 0).start()

                return carry
            for side, hops in ((0, LONG), (1, SHORT)):
                if step >= hops:
                    continue
                sign = (1 - 2 * lax.rem(v, 2)) * (1 - 2 * side)
                to = lax.rem(z + ZS + sign * (hops - step), ZS)
                both = z_local(v, 0, to)
                if step > 0:
                    z_hop(v, side, step - 1).wait_recv()
                    both = both + zrecv[v, side, step].astype(F32)
                zsend[v, side, step] = both.astype(BF16)
                z_hop(v, side, step).start()
            return carry

        return run

    def x_step(step):
        def run(u, carry):
            slot, way = u, 1
            sign = 1 - 2 * lax.rem(u, 2)
            if step == 0:
                xsend[u, 0] = x_local(slot, way, lax.rem(x + 2, XS)).astype(BF16)
                x_hop(u, 0).start()
                xsend[u, 2] = x_local(slot, way, lax.rem(x + XS - sign, XS)).astype(BF16)
                x_hop(u, 2).start()
                return carry
            if step == 1:
                mine = x_local(slot, way, lax.rem(x + XS + sign, XS))
                x_hop(u, 0).wait_recv()
                xsend[u, 1] = (mine + xrecv[u, 0].astype(F32)).astype(BF16)
                x_hop(u, 1).start()
                return carry
            if step == 3:
                for kind in range(3):
                    z_pass(u, kind).wait_recv()
                extra = z_passed[u, 2].astype(F32)
                for side in range(2):
                    total = z_owed[u, z_at((2, -2)[side])].astype(F32)
                    total = total + z_passed[u, side].astype(F32)
                    total = total + jnp.where(lax.rem(u, 2) == side, extra, 0.0)
                    z_joined[u, side] = total.astype(BF16)
                    z_owe(u, 3 + side).start()
                return carry
            total = x_local(slot, way, x)
            x_hop(u, 1).wait_recv()
            x_hop(u, 2).wait_recv()
            total = total + xrecv[u, 1].astype(F32) + xrecv[u, 2].astype(F32)
            z_owed[u] = total.astype(BF16).reshape(ZS, OUT, 2 * HEAD)
            for kind in (2, 0, 1):
                z_pass(u, kind).start()
            for kind in (1, 2):
                z_owe(u, kind).start()

            @pl.when(u == 0)
            def _():
                z_arrived[0, 0] = z_owed[0, z]

            @pl.when(u > 0)
            def _():
                z_owe(u, 0).start()

            return carry

        return run

    for kind, step, first, end in ORDER:
        if kind == "x":
            lax.fori_loop(first, end, x_step(step), 0)
        elif kind == "z":
            lax.fori_loop(first, end, z_step(step), 0)
        else:
            layer_relay(step).wait_recv()
            turn(3, step)
    for e in range(2):
        for k in range(1, ZS):
            z_copy(e, k).wait_send()
        for k in range(1, XS):
            x_copy(e, k).wait_send()
    for half in range(2):
        for slot in (1, 2):
            layer_copy(slot, half).wait_send()
        layer_relay(half).wait_send()
    swap.wait_send()

    def drain(u, carry):
        for side, hops in ((0, LONG), (1, SHORT)):
            for step in range(hops):
                z_hop(u, side, step).wait_send()
        for kind in range(3):
            x_hop(u, kind).wait_send()
            z_pass(u, kind).wait_send()
        return carry

    lax.fori_loop(0, YS, drain, 0)
    grad_copy.wait()
    for slot in range(YS):
        source = lax.rem(y + YS - (0, 1, 3, 2)[slot], YS) * 2
        for way in range(2):
            first = 0 if slot else 1
            if way == 0:
                for k in range(first, XS):
                    x_owe(slot, k).wait_recv()
                pieces = [x_arrived[slot, k] for k in range(XS)]
            else:
                for kind in range(first, NEAR):
                    z_owe(slot, kind).wait_recv()
                pieces = [z_arrived[slot, kind] for kind in range(NEAR)]
            total = pieces[0].astype(F32)
            for piece in pieces[1:]:
                total = total + piece.astype(F32)
            column = columns(source + way)
            key_out[:, column] = total[:, 0:HEAD]
            value_out[:, column] = total[:, HEAD : 2 * HEAD]

    def drain_last(u, carry):
        for k in range(1, XS):
            x_owe(u, k).wait_send()
        for kind in range(1, NEAR):
            z_owe(u, kind).wait_send()

        @pl.when(u > 0)
        def _():
            x_owe(u, 0).wait_send()
            z_owe(u, 0).wait_send()

        return carry

    lax.fori_loop(0, YS, drain_last, 0)


def shards(layer_input, query_columns, key_columns, value_columns, output_gradient):
    shape = jax.ShapeDtypeStruct
    vmem = pltpu.VMEM
    sems = pltpu.SemaphoreType.DMA
    wide = GROUP * HEAD
    far = pl.BlockSpec(memory_space=pl.ANY)
    near = pl.BlockSpec(memory_space=pltpu.VMEM)
    return pl.pallas_call(
        kernel,
        out_shape=(
            shape((ROWS, wide), BF16),
            shape((OUT, KEY_VALUE_HEADS * HEAD), F32),
            shape((OUT, KEY_VALUE_HEADS * HEAD), F32),
        ),
        in_specs=[far] * 5,
        out_specs=(far, near, near),
        scratch_shapes=[
            vmem((ROWS, wide), BF16),
            vmem((ROWS, wide), BF16),
            vmem((ROWS, HEAD), BF16),
            vmem((ROWS, HEAD), BF16),
            vmem((YS, ROWS, wide), BF16),
            vmem((ROWS, HEAD), BF16),
            vmem((ROWS, HEAD), F32),
            vmem((2, HEAD, HEAD), F32),
            vmem((2, 8, HEAD), F32),
            vmem((2, HEAD, HEAD), BF16),
            vmem((2, HEAD, HEAD), BF16),
            vmem((2, 8, HEAD), F32),
            vmem((HEAD + 8, HEAD), F32),
            vmem((ROWS, wide), BF16),
            vmem((GROUP, 2, BLOCK, BLOCK), BF16),
            vmem((ROWS, wide), F32),
            vmem((ROWS, wide), BF16),
            vmem((ROWS, wide), F32),
            vmem((ROWS, wide), BF16),
            vmem((2, HEAD, HEAD), F32),
            vmem((2, 8, HEAD), F32),
            vmem((ROWS, HEAD), F32),
            vmem((ROWS, HEAD), F32),
            vmem((2, 2, MESSAGE, HEAD), BF16),
            vmem((2, ZS, MESSAGE, HEAD), BF16),
            vmem((2, XS, MESSAGE, HEAD), BF16),
            vmem((YS, ZS, XS, OUT, ROWS), BF16),
            vmem((2, ROWS, 2 * HEAD), BF16),
            vmem((YS, 2, LONG, XS * OUT, 2 * HEAD), BF16),
            vmem((YS, 2, LONG + 1, XS * OUT, 2 * HEAD), BF16),
            vmem((YS, 3, ZS * OUT, 2 * HEAD), BF16),
            vmem((YS, 3, ZS * OUT, 2 * HEAD), BF16),
            vmem((YS, XS, OUT, 2 * HEAD), BF16),
            vmem((YS, ZS, OUT, 2 * HEAD), BF16),
            vmem((YS, XS, OUT, 2 * HEAD), BF16),
            vmem((YS, NEAR, OUT, 2 * HEAD), BF16),
            vmem((YS, 3, OUT, 2 * HEAD), BF16),
            vmem((YS, 2, OUT, 2 * HEAD), BF16),
            sems((6,)),
            sems((2, ZS)),
            sems((2, ZS)),
            sems((2, XS)),
            sems((2, XS)),
            sems((YS, 2)),
            sems((YS, 2)),
            sems((1,)),
            sems((1,)),
            sems((YS, 2, LONG)),
            sems((YS, 2, LONG + 1)),
            sems((YS, 3)),
            sems((YS, 3)),
            sems((YS, XS)),
            sems((YS, XS)),
            sems((YS, NEAR)),
            sems((YS, NEAR)),
            sems((YS, 3)),
            sems((YS, 3)),
        ],
        compiler_params=pltpu.CompilerParams(
            collective_id=0, has_side_effects=True, vmem_limit_bytes=LIMIT
        ),
        name="backward",
    )(query_columns, output_gradient, key_columns, value_columns, layer_input)


def solution(mesh):
    placed = (P("ctx", "head"),) * 5
    return jax.shard_map(
        shards,
        mesh=mesh,
        in_specs=placed,
        out_specs=(P("ctx", "head"), P(("head", "ctx"), None), P(("head", "ctx"), None)),
        check_vma=False,
    )
```

```python
import jax
import jax.numpy as jnp
from jax import lax
from jax.experimental import pallas as pl
from jax.experimental.pallas import tpu as pltpu
from jax.sharding import PartitionSpec as P

QUERY_HEADS = 64
KEY_VALUE_HEADS = 8
GROUP = QUERY_HEADS // KEY_VALUE_HEADS
HEAD = 128
BLOCK = 256
ROWS = 512
XS = 4
ZS = 8
YS = 4
OUT = 32
MESSAGE = HEAD + 16
MESH = pl.DeviceIdType.MESH
F32 = jnp.float32
BF16 = jnp.bfloat16
HALF = 512
LONG = 4
SHORT = 3
NEAR = 5
ORDER = (
    ("x", 0, 0, 1),
    ("z", 0, 0, 1),
    ("x", 0, 1, 2),
    ("z", 0, 1, 2),
    ("x", 0, 2, 3),
    ("z", 0, 2, 3),
    ("turn", 0, 0, 0),
    ("z", 1, 0, 3),
    ("x", 1, 0, 2),
    ("turn", 1, 0, 0),
    ("z", 0, 3, 4),
    ("x", 0, 3, 4),
    ("x", 1, 2, 3),
    ("z", 2, 0, 3),
    ("z", 1, 3, 4),
    ("x", 2, 0, 3),
    ("x", 1, 3, 4),
    ("z", 3, 0, 3),
    ("z", 2, 3, 4),
    ("x", 3, 0, 3),
    ("x", 2, 3, 4),
    ("z", 4, 0, 3),
    ("z", 3, 3, 4),
    ("x", 3, 3, 4),
    ("z", 4, 3, 4),
)
EARLY = 6
LIMIT = 52 << 20


def phi(raw):
    wide = raw.astype(F32)
    return jnp.where(wide > 0, wide + 1.0, jnp.exp(jnp.minimum(wide, 0.0))).astype(BF16)


def slope(raw):
    wide = raw.astype(F32)
    return jnp.where(wide > 0, 1.0, jnp.exp(jnp.minimum(wide, 0.0)))


def dot_nn(a, b):
    return lax.dot_general(a, b, (((1,), (0,)), ((), ())), preferred_element_type=F32)


def dot_nt(a, b):
    return lax.dot_general(a, b, (((1,), (1,)), ((), ())), preferred_element_type=F32)


def dot_tn(a, b):
    return lax.dot_general(a, b, (((0,), (0,)), ((), ())), preferred_element_type=F32)


def halves(value):
    high = value.astype(BF16)
    return high, (value - high.astype(F32)).astype(BF16)


def lower_mask():
    rows = lax.broadcasted_iota(jnp.int32, (BLOCK, BLOCK), 0)
    cols = lax.broadcasted_iota(jnp.int32, (BLOCK, BLOCK), 1)
    return cols <= rows


def remote(source, target, send, recv, device):
    return pltpu.make_async_remote_copy(
        src_ref=source,
        dst_ref=target,
        send_sem=send,
        recv_sem=recv,
        device_id=device,
        device_id_type=MESH,
    )


def pack(target, state, total):
    target[0:HEAD, :] = state.astype(BF16)
    high, low = halves(total)
    row = lax.broadcasted_iota(jnp.int32, (16, HEAD), 0)
    tail = jnp.where(row == 0, high.astype(F32), jnp.where(row == 1, low.astype(F32), 0.0))
    target[HEAD:MESSAGE, :] = tail.astype(BF16)


def parts(message):
    return message[0:HEAD, :], message[HEAD : HEAD + 1, :] + message[HEAD + 1 : HEAD + 2, :]


def kernel(
    query_hbm, cotangent_hbm, key_hbm, value_hbm, layer_hbm,
    query_grad_hbm, key_out, value_out,
    query, cotangent, key, value, layer,
    features, sums, states, totals, high, low, prior_total, rowsum,
    qf_all, scores_all, numer_all, g_all, c_all, grad_all,
    gstate, gtotal, dkey, dvalue,
    message, from_z, from_x,
    turned, paired, zsend, zrecv, xsend, xrecv, x_owed, z_owed, x_arrived, z_arrived, z_passed, z_joined,
    load, zs, zr, xs, xr, l_send, l_recv, f_send, f_recv,
    p_send, p_recv, q_send, q_recv, x_send, x_recv, z_send, z_recv, m_send, m_recv,
):
    me = lax.axis_index("ctx")
    head = lax.axis_index("head")
    x = me // ZS
    z = lax.rem(me, ZS)
    y = head // 2
    core = lax.rem(head, 2)
    sibling = {"head": head + 1 - 2 * core}
    z_line = [{"ctx": x * ZS + lax.rem(z + k, ZS)} for k in range(ZS)]
    x_line = [{"ctx": lax.rem(x + k, XS) * ZS + z} for k in range(XS)]
    y_line = [{"head": lax.rem(y + k, YS) * 2 + core} for k in range(YS)]

    loads = [
        pltpu.make_async_copy(source, target, load.at[i])
        for i, (source, target) in enumerate(
            (
                (key_hbm, key),
                (value_hbm, value),
                (query_hbm, query),
                (cotangent_hbm, cotangent),
                (layer_hbm, layer.at[0]),
            )
        )
    ]
    loads[0].start()
    loads[1].start()
    barrier = pltpu.get_barrier_semaphore()
    for device in z_line[1:] + x_line[1:] + y_line[1:] + [sibling]:
        pl.semaphore_signal(barrier, inc=1, device_id=device, device_id_type=MESH)
    for copy in loads[2:]:
        copy.start()

    def z_copy(e, k):
        return remote(message.at[e, 0], from_z.at[e, k], zs.at[e, k], zr.at[e, k], z_line[k])

    def x_copy(e, k):
        return remote(message.at[e, 1], from_x.at[e, k], xs.at[e, k], xr.at[e, k], x_line[k])

    def z_finish(e, state, total, reverse):
        line_state, line_total = state, total
        part_state, part_total = jnp.zeros_like(state), jnp.zeros_like(total)
        for k in range(1, ZS):
            z_copy(e, k).wait_recv()
            got_state, got_total = parts(from_z[e, k].astype(F32))
            line_state, line_total = line_state + got_state, line_total + got_total
            counts = (k > z) if reverse else (k <= z)
            part_state = part_state + jnp.where(counts, got_state, 0.0)
            part_total = part_total + jnp.where(counts, got_total, 0.0)
        pack(message.at[e, 1], line_state, line_total)
        for k in range(1, XS):
            x_copy(e, k).start()
        rowsum[0:HEAD, :] = part_state
        rowsum[HEAD : HEAD + 8, :] = jnp.broadcast_to(part_total, (8, HEAD))

    def x_finish(e, reverse):
        state, total = rowsum[0:HEAD, :], rowsum[HEAD : HEAD + 1, :]
        for k in range(1, XS):
            x_copy(e, k).wait_recv()
            got_state, got_total = parts(from_x[e, k].astype(F32))
            counts = (k > x) if reverse else (k <= x)
            state = state + jnp.where(counts, got_state, 0.0)
            total = total + jnp.where(counts, got_total, 0.0)
        return state, total

    mask = lower_mask()
    blocks = [pl.ds(b * BLOCK, BLOCK) for b in range(2)]

    loads[0].wait()
    loads[1].wait()
    for b in range(2):
        kf = phi(key[blocks[b], :])
        features[blocks[b], :] = kf
        states[b] = dot_tn(kf, value[blocks[b], :])
        totals[b] = jnp.broadcast_to(
            jnp.sum(kf.astype(F32), axis=0, keepdims=True), (8, HEAD)
        )
    own_total = totals[0, 0:1, :] + totals[1, 0:1, :]
    pack(message.at[0, 0], states[0] + states[1], own_total)
    pl.semaphore_wait(barrier, ZS - 1 + XS - 1 + YS - 1 + 1)
    for k in range(1, ZS):
        z_copy(0, k).start()

    def layer_copy(slot, half):
        part = pl.ds(half * HALF, HALF)
        return remote(
            layer.at[0, :, part],
            layer.at[slot, :, part],
            l_send.at[slot, half],
            l_recv.at[slot, half],
            y_line[YS - 1 if slot == 1 else 1],
        )

    def layer_relay(half):
        part = pl.ds(half * HALF, HALF)
        return remote(
            layer.at[1 + core, :, part],
            layer.at[3, :, part],
            l_send.at[3, half],
            l_recv.at[3, half],
            {"head": lax.rem(y + YS - 1 + 2 * core, YS) * 2 + core},
        )

    def turn(slot, half):
        def one(i, carry):
            j = half * 4 + i
            block = layer[slot, :, pl.ds(pl.multiple_of(j * HEAD, HEAD), HEAD)].T
            for q in range(4):
                turned[slot, lax.rem(j, 2) * 4 + q, j // 2] = block[q * OUT : (q + 1) * OUT, :]
            return carry

        lax.fori_loop(0, 4, one, 0)

    loads[4].wait()
    for slot in (1, 2):
        layer_copy(slot, 0).start()

    triangle = jnp.where(mask, 1.0, 0.0).astype(BF16)
    for b in range(2):
        sums[blocks[b], :] = dot_nn(triangle, features[blocks[b], :])
    gstate[...] = jnp.zeros_like(gstate)
    gtotal[...] = jnp.zeros_like(gtotal)
    dkey[...] = jnp.zeros_like(dkey)
    dvalue[...] = jnp.zeros_like(dvalue)

    def columns(h):
        return pl.ds(pl.multiple_of(h * HEAD, HEAD), HEAD)

    def inside(h, carry):
        at = columns(h)
        for b in range(2):
            qf = phi(query[blocks[b], at])
            qf_all[blocks[b], at] = qf
            scores = jnp.where(mask, dot_nt(qf, features[blocks[b], :]), 0.0).astype(BF16)
            scores_all[h, b] = scores
            numer_all[blocks[b], at] = dot_nn(scores, value[blocks[b], :])
        return carry

    def forward_pass(h, carry):
        at = columns(h)
        for b in range(2):
            qf = qf_all[blocks[b], at]
            wide = qf.astype(F32)
            den = jnp.sum(wide * sums[blocks[b], :], axis=1, keepdims=True)
            numer = numer_all[blocks[b], at] + dot_nn(qf, high[b]) + dot_nn(qf, low[b])
            inverse = 1.0 / den
            wide_cot = cotangent[blocks[b], at].astype(F32)
            g = (wide_cot * inverse).astype(BF16)
            c = -jnp.sum(wide_cot * numer, axis=1, keepdims=True) * inverse * inverse
            c = jnp.broadcast_to(c, (BLOCK, HEAD))
            g_all[blocks[b], at] = g
            c_all[blocks[b], at] = c
            gstate[b] += dot_tn(qf, g)
            gtotal[b] += jnp.broadcast_to(jnp.sum(wide * c, axis=0, keepdims=True), (8, HEAD))
        return carry

    def backward_pass(h, carry):
        at = columns(h)
        for b in range(2):
            g = g_all[blocks[b], at]
            qf = qf_all[blocks[b], at]
            c = c_all[blocks[b], at]
            kf = features[blocks[b], :]
            dscores = dot_nt(g, value[blocks[b], :]) + jnp.concatenate([c, c], axis=1)
            dscores = jnp.where(mask, dscores, 0.0).astype(BF16)
            dqf = (
                dot_nt(g, high[b])
                + dot_nt(g, low[b])
                + c * prior_total[b, 0:1, :]
                + dot_nn(dscores, kf)
            )
            grad_all[blocks[b], at] = (dqf * slope(query[blocks[b], at])).astype(BF16)
            dkey[blocks[b], :] += dot_tn(dscores, qf)
            dvalue[blocks[b], :] += dot_tn(scores_all[h, b], g)
        return carry

    loads[2].wait()
    lax.fori_loop(0, GROUP // 2, inside, 0)
    z_finish(0, states[0] + states[1], own_total, False)
    for slot in (1, 2):
        layer_copy(slot, 1).start()
    lax.fori_loop(GROUP // 2, GROUP, inside, 0)
    turn(0, 0)
    turn(0, 1)
    loads[3].wait()
    state, total = x_finish(0, False)
    for b in range(2):
        high[b], low[b] = halves(state)
        prior_total[b] = jnp.broadcast_to(total, (8, HEAD))
        sums[blocks[b], :] += total
        state = state + states[b]
        total = total + totals[b, 0:1, :]
    lax.fori_loop(0, GROUP, forward_pass, 0, unroll=2)
    own_gtotal = gtotal[0, 0:1, :] + gtotal[1, 0:1, :]
    pack(message.at[1, 0], gstate[0] + gstate[1], own_gtotal)
    for k in range(1, ZS):
        z_copy(1, k).start()
    for slot in (1, 2):
        layer_copy(slot, 0).wait_recv()
    layer_relay(0).start()
    lax.fori_loop(0, EARLY, backward_pass, 0)
    turn(1, 0)
    turn(2, 0)
    z_finish(1, gstate[0] + gstate[1], own_gtotal, True)
    lax.fori_loop(EARLY, GROUP, backward_pass, 0)
    grad_copy = pltpu.make_async_copy(grad_all, query_grad_hbm, load.at[5])
    grad_copy.start()
    for slot in (1, 2):
        layer_copy(slot, 1).wait_recv()
    layer_relay(1).start()
    turn(1, 1)
    turn(2, 1)
    later, later_total = x_finish(1, True)
    for b in (1, 0):
        later_high, later_low = halves(later)
        v = value[blocks[b], :]
        kf = features[blocks[b], :]
        dk = dkey[blocks[b], :] + dot_nt(v, later_high) + dot_nt(v, later_low) + later_total
        paired[core, blocks[b], 0:HEAD] = (dk * slope(key[blocks[b], :])).astype(BF16)
        dv = dvalue[blocks[b], :] + dot_nn(kf, later_high) + dot_nn(kf, later_low)
        paired[core, blocks[b], HEAD : 2 * HEAD] = dv.astype(BF16)
        later = later + gstate[b]
        later_total = later_total + gtotal[b, 0:1, :]

    swap = remote(paired.at[core], paired.at[core], f_send.at[0], f_recv.at[0], sibling)
    swap_in = remote(paired.at[1 - core], paired.at[1 - core], f_send.at[0], f_recv.at[0], sibling)
    swap.start()
    swap_in.wait_recv()

    def away_of(slot):
        return slot + (slot // 2) * (1 - 2 * lax.rem(slot, 2))

    def z_local(slot, way, to):
        return dot_nn(turned[slot, to].reshape(XS * OUT, ROWS), paired[way])

    def x_local(slot, way, to):
        return dot_nn(turned[slot, :, to].reshape(ZS * OUT, ROWS), paired[way])

    def z_hop(v, side, step):
        sign = (1 - 2 * lax.rem(v, 2)) * (1 - 2 * side)
        return remote(
            zsend.at[v, side, step],
            zrecv.at[v, side, step + 1],
            p_send.at[v, side, step],
            p_recv.at[v, side, step + 1],
            {"ctx": x * ZS + lax.rem(z + ZS + sign, ZS)},
        )

    def x_hop(u, kind):
        sign = 1 - 2 * lax.rem(u, 2)
        if kind == 2:
            sign = -sign
        return remote(
            xsend.at[u, kind],
            xrecv.at[u, kind],
            q_send.at[u, kind],
            q_recv.at[u, kind],
            {"ctx": lax.rem(x + XS + sign, XS) * ZS + z},
        )

    def x_owe(v, k):
        to = lax.rem(x + k, XS)
        return remote(
            x_owed.at[v, to],
            x_arrived.at[v, k],
            x_send.at[v, k],
            x_recv.at[v, k],
            {"ctx": to * ZS + z, "head": lax.rem(y + away_of(v), YS) * 2 + core},
        )

    def z_at(k):
        return lax.rem(z + ZS + k, ZS)

    def z_owe(u, kind):
        if kind < 3:
            to = z_at((0, 1, -1)[kind])
            source = z_owed.at[u, to]
        else:
            to = z_at((2, -2)[kind - 3])
            source = z_joined.at[u, kind - 3]
        return remote(
            source,
            z_arrived.at[u, kind],
            z_send.at[u, kind],
            z_recv.at[u, kind],
            {"ctx": x * ZS + to, "head": lax.rem(y + away_of(u), YS) * 2 + core},
        )

    def z_pass(u, kind):
        sign = 1 - 2 * lax.rem(u, 2)
        chunk = z_at((3, -3, 4)[kind])
        to = z_at((1, -1, 2 * sign)[kind])
        return remote(
            z_owed.at[u, chunk],
            z_passed.at[u, kind],
            m_send.at[u, kind],
            m_recv.at[u, kind],
            {"ctx": x * ZS + to},
        )

    def z_step(step):
        def run(v, carry):
            if step == LONG:
                total = z_local(v, 0, z)
                z_hop(v, 0, LONG - 1).wait_recv()
                z_hop(v, 1, SHORT - 1).wait_recv()
                total = total + zrecv[v, 0, LONG].astype(F32) + zrecv[v, 1, SHORT].astype(F32)
                x_owed[v] = total.astype(BF16).reshape(XS, OUT, 2 * HEAD)
                for k in range(1, XS):
                    x_owe(v, k).start()

                @pl.when(v == 0)
                def _():
                    x_arrived[0, 0] = x_owed[0, x]

                @pl.when(v > 0)
                def _():
                    x_owe(v, 0).start()

                return carry
            for side, hops in ((0, LONG), (1, SHORT)):
                if step >= hops:
                    continue
                sign = (1 - 2 * lax.rem(v, 2)) * (1 - 2 * side)
                to = lax.rem(z + ZS + sign * (hops - step), ZS)
                both = z_local(v, 0, to)
                if step > 0:
                    z_hop(v, side, step - 1).wait_recv()
                    both = both + zrecv[v, side, step].astype(F32)
                zsend[v, side, step] = both.astype(BF16)
                z_hop(v, side, step).start()
            return carry

        return run

    def x_step(step):
        def run(u, carry):
            slot, way = u, 1
            sign = 1 - 2 * lax.rem(u, 2)
            if step == 0:
                xsend[u, 0] = x_local(slot, way, lax.rem(x + 2, XS)).astype(BF16)
                x_hop(u, 0).start()
                xsend[u, 2] = x_local(slot, way, lax.rem(x + XS - sign, XS)).astype(BF16)
                x_hop(u, 2).start()
                return carry
            if step == 1:
                mine = x_local(slot, way, lax.rem(x + XS + sign, XS))
                x_hop(u, 0).wait_recv()
                xsend[u, 1] = (mine + xrecv[u, 0].astype(F32)).astype(BF16)
                x_hop(u, 1).start()
                return carry
            if step == 3:
                for kind in range(3):
                    z_pass(u, kind).wait_recv()
                extra = z_passed[u, 2].astype(F32)
                for side in range(2):
                    total = z_owed[u, z_at((2, -2)[side])].astype(F32)
                    total = total + z_passed[u, side].astype(F32)
                    total = total + jnp.where(lax.rem(u, 2) == side, extra, 0.0)
                    z_joined[u, side] = total.astype(BF16)
                    z_owe(u, 3 + side).start()
                return carry
            total = x_local(slot, way, x)
            x_hop(u, 1).wait_recv()
            x_hop(u, 2).wait_recv()
            total = total + xrecv[u, 1].astype(F32) + xrecv[u, 2].astype(F32)
            z_owed[u] = total.astype(BF16).reshape(ZS, OUT, 2 * HEAD)
            for kind in (2, 0, 1):
                z_pass(u, kind).start()
            for kind in (1, 2):
                z_owe(u, kind).start()

            @pl.when(u == 0)
            def _():
                z_arrived[0, 0] = z_owed[0, z]

            @pl.when(u > 0)
            def _():
                z_owe(u, 0).start()

            return carry

        return run

    for kind, step, first, end in ORDER:
        if kind == "x":
            lax.fori_loop(first, end, x_step(step), 0)
        elif kind == "z":
            lax.fori_loop(first, end, z_step(step), 0)
        else:
            layer_relay(step).wait_recv()
            turn(3, step)
    for e in range(2):
        for k in range(1, ZS):
            z_copy(e, k).wait_send()
        for k in range(1, XS):
            x_copy(e, k).wait_send()
    for half in range(2):
        for slot in (1, 2):
            layer_copy(slot, half).wait_send()
        layer_relay(half).wait_send()
    swap.wait_send()

    def drain(u, carry):
        for side, hops in ((0, LONG), (1, SHORT)):
            for step in range(hops):
                z_hop(u, side, step).wait_send()
        for kind in range(3):
            x_hop(u, kind).wait_send()
            z_pass(u, kind).wait_send()
        return carry

    lax.fori_loop(0, YS, drain, 0)
    grad_copy.wait()
    for slot in range(YS):
        source = lax.rem(y + YS - (0, 1, 3, 2)[slot], YS) * 2
        for way in range(2):
            first = 0 if slot else 1
            if way == 0:
                for k in range(first, XS):
                    x_owe(slot, k).wait_recv()
                pieces = [x_arrived[slot, k] for k in range(XS)]
            else:
                for kind in range(first, NEAR):
                    z_owe(slot, kind).wait_recv()
                pieces = [z_arrived[slot, kind] for kind in range(NEAR)]
            total = pieces[0].astype(F32)
            for piece in pieces[1:]:
                total = total + piece.astype(F32)
            column = columns(source + way)
            key_out[:, column] = total[:, 0:HEAD]
            value_out[:, column] = total[:, HEAD : 2 * HEAD]

    def drain_last(u, carry):
        for k in range(1, XS):
            x_owe(u, k).wait_send()
        for kind in range(1, NEAR):
            z_owe(u, kind).wait_send()

        @pl.when(u > 0)
        def _():
            x_owe(u, 0).wait_send()
            z_owe(u, 0).wait_send()

        return carry

    lax.fori_loop(0, YS, drain_last, 0)


def shards(layer_input, query_columns, key_columns, value_columns, output_gradient):
    shape = jax.ShapeDtypeStruct
    vmem = pltpu.VMEM
    sems = pltpu.SemaphoreType.DMA
    wide = GROUP * HEAD
    far = pl.BlockSpec(memory_space=pl.ANY)
    near = pl.BlockSpec(memory_space=pltpu.VMEM)
    return pl.pallas_call(
        kernel,
        out_shape=(
            shape((ROWS, wide), BF16),
            shape((OUT, KEY_VALUE_HEADS * HEAD), F32),
            shape((OUT, KEY_VALUE_HEADS * HEAD), F32),
        ),
        in_specs=[far] * 5,
        out_specs=(far, near, near),
        scratch_shapes=[
            vmem((ROWS, wide), BF16),
            vmem((ROWS, wide), BF16),
            vmem((ROWS, HEAD), BF16),
            vmem((ROWS, HEAD), BF16),
            vmem((YS, ROWS, wide), BF16),
            vmem((ROWS, HEAD), BF16),
            vmem((ROWS, HEAD), F32),
            vmem((2, HEAD, HEAD), F32),
            vmem((2, 8, HEAD), F32),
            vmem((2, HEAD, HEAD), BF16),
            vmem((2, HEAD, HEAD), BF16),
            vmem((2, 8, HEAD), F32),
            vmem((HEAD + 8, HEAD), F32),
            vmem((ROWS, wide), BF16),
            vmem((GROUP, 2, BLOCK, BLOCK), BF16),
            vmem((ROWS, wide), F32),
            vmem((ROWS, wide), BF16),
            vmem((ROWS, wide), F32),
            vmem((ROWS, wide), BF16),
            vmem((2, HEAD, HEAD), F32),
            vmem((2, 8, HEAD), F32),
            vmem((ROWS, HEAD), F32),
            vmem((ROWS, HEAD), F32),
            vmem((2, 2, MESSAGE, HEAD), BF16),
            vmem((2, ZS, MESSAGE, HEAD), BF16),
            vmem((2, XS, MESSAGE, HEAD), BF16),
            vmem((YS, ZS, XS, OUT, ROWS), BF16),
            vmem((2, ROWS, 2 * HEAD), BF16),
            vmem((YS, 2, LONG, XS * OUT, 2 * HEAD), BF16),
            vmem((YS, 2, LONG + 1, XS * OUT, 2 * HEAD), BF16),
            vmem((YS, 3, ZS * OUT, 2 * HEAD), BF16),
            vmem((YS, 3, ZS * OUT, 2 * HEAD), BF16),
            vmem((YS, XS, OUT, 2 * HEAD), BF16),
            vmem((YS, ZS, OUT, 2 * HEAD), BF16),
            vmem((YS, XS, OUT, 2 * HEAD), BF16),
            vmem((YS, NEAR, OUT, 2 * HEAD), BF16),
            vmem((YS, 3, OUT, 2 * HEAD), BF16),
            vmem((YS, 2, OUT, 2 * HEAD), BF16),
            sems((6,)),
            sems((2, ZS)),
            sems((2, ZS)),
            sems((2, XS)),
            sems((2, XS)),
            sems((YS, 2)),
            sems((YS, 2)),
            sems((1,)),
            sems((1,)),
            sems((YS, 2, LONG)),
            sems((YS, 2, LONG + 1)),
            sems((YS, 3)),
            sems((YS, 3)),
            sems((YS, XS)),
            sems((YS, XS)),
            sems((YS, NEAR)),
            sems((YS, NEAR)),
            sems((YS, 3)),
            sems((YS, 3)),
        ],
        compiler_params=pltpu.CompilerParams(
            collective_id=0, has_side_effects=True, vmem_limit_bytes=LIMIT
        ),
        name="backward",
    )(query_columns, output_gradient, key_columns, value_columns, layer_input)


def solution(mesh):
    placed = (P("ctx", "head"),) * 5
    return jax.shard_map(
        shards,
        mesh=mesh,
        in_specs=placed,
        out_specs=(P("ctx", "head"), P(("head", "ctx"), None), P(("head", "ctx"), None)),
        check_vma=False,
    )
```
